128 devices in a mesh: dp: 8 (over z, y_lo), shard: 16 (over x, y_hi, core).
Axes of the slice: x: 4, y: 4 (y_hi: 2, y_lo: 2; y = y_hi * 2 + y_lo), z: 4, core: 2. Of those that a mesh axis runs over, the one named last changes fastest.
Arguments:
- prefill_x: bfloat16 [98304, 1536], P(('dp', 'shard')), may hold values from -6 to 6
- decode_x: bfloat16 [64, 1536], P('dp'), may hold values from -6 to 6
- norm_gain: bfloat16 [1536], P(('dp', 'shard')), may hold values from 0.099609375 to 1.8984375
- wqkv: bfloat16 [1536, 3072], P(('dp', 'shard')), may hold values from -0.15625 to 0.15625
- wo: bfloat16 [1536, 1536], P(('dp', 'shard')), may hold values from -0.15625 to 0.15625
- k_cache: bfloat16 [64, 8192, 768], P('dp', 'shard'), may hold values from -360 to 360
- v_cache: bfloat16 [64, 8192, 768], P('dp', 'shard'), may hold values from -6 to 6
- cache_len: int32 [64], P('dp'), may hold values from 1 to 8192, as said below
Outputs:
- prefill_out: bfloat16 [98304, 1536], P(('dp', 'shard'))
- decode_out: bfloat16 [64, 1536], P('dp')
The draws below stay inside these ranges and needn't reach their ends.
Inputs may be any that keep to these rules, and one draw needn't show every extreme that they name: `cache_len`: some request has exactly 8192 cached positions.
All inputs are finite; a program needn't handle non-finite values.
Results may differ from the reference program's by a relative error of at most 0.0095.
The reference program's roundings to bfloat16 on the way count: a program that leaves them out, or rounds other values in their place, can miss the bound.
Values may be sent and summed in bfloat16 or wider, within the bound.
A program may use at most 128 MiB of HBM per device.

```python
import jax
import jax.numpy as jnp
from jax import lax

D = 1536
H = 16
KV = 8
HD = 96
STRETCH = 768
CL_DEV = 512
QKVW = 3072
CACHE = 8192
REQS = 64
TOKENS = 98304
N_SHARD = 16


def draw_k_cache(key, part):
    left_key = jax.random.fold_in(key, 0)
    drawn = jax.random.truncated_normal(left_key, -6.0, 6.0, (REQS, CACHE, KV * HD), jnp.float32) * 2.0
    return drawn.astype(jnp.bfloat16)


def draw_cache_len(key, part):
    left_key, right_key = jax.random.split(key)
    lengths = jax.random.randint(left_key, (REQS,), 1, CACHE + 1)
    chosen = jax.random.randint(right_key, (), 0, REQS)
    return jnp.where(jnp.arange(REQS) == chosen, CACHE, lengths).astype(jnp.int32)


def block_levels(key, dims, cuts, least, top_value):
    loudness, own = 1.0, jax.random.fold_in(key, 6)
    for position, shards_of in cuts:
        heights = jnp.exp(jax.random.uniform(jax.random.fold_in(own, position), (shards_of,), jnp.float32, least / len(cuts), top_value / len(cuts)))
        loudness = loudness * jnp.repeat(heights, dims[position] // shards_of).reshape([-1 if axis == position else 1 for axis in range(len(dims))])
    return loudness


def bell_draw(key, dims, spread, bound, cuts=(), kind=jnp.bfloat16):
    entries = spread * jax.random.normal(key, dims, jnp.float32)
    if cuts:
        entries = entries * block_levels(key, dims, cuts, -0.22, 0.18)
    return jnp.clip(entries, -bound, bound).astype(kind)


def setup_inputs(seed: int = 0) -> dict:
    keys = jax.random.split(jax.random.key(seed), 9)
    prefill_x = bell_draw(keys[0], (TOKENS, D), 1.0, 6.0, ((0, 128),))
    decode_x = bell_draw(keys[1], (REQS, D), 1.0, 6.0, ((0, 8),))
    norm_gain = jnp.clip(1.0 + 0.18 * jax.random.normal(keys[2], (D,), jnp.float32), 0.099609375, 1.8984375).astype(jnp.bfloat16)
    wqkv = bell_draw(keys[3], (D, QKVW), D ** -0.5, 0.15625, ((0, 128),))
    wo = bell_draw(keys[4], (D, D), D ** -0.5, 0.15625, ((0, 128),))
    k_cache = draw_k_cache(jax.random.fold_in(keys[8], 71), 0)
    v_cache = bell_draw(keys[6], (REQS, CACHE, KV * HD), 1.0, 6.0, ((0, 8), (1, 16)))
    cache_len = draw_cache_len(jax.random.fold_in(keys[8], 71), 0)
    return {"prefill_x": prefill_x, "decode_x": decode_x, "norm_gain": norm_gain, "wqkv": wqkv, "wo": wo, "k_cache": k_cache, "v_cache": v_cache, "cache_len": cache_len}


THETA = 100000.0
EPS = 1e-05
NEGATIVE = -1e+30

def normalize(inputs, norm_gain):
    widened = inputs.astype(jnp.float32)
    factor = lax.rsqrt(lax.optimization_barrier(jnp.mean(widened * widened, axis=-1, keepdims=True)) + EPS)
    return (widened * factor * norm_gain.astype(jnp.float32)).astype(jnp.bfloat16)

def rotate(tensor, positions):
    half_width = tensor.shape[-1] // 2
    frequency = jnp.power(THETA, -jnp.arange(half_width, dtype=jnp.float32) * (2.0 / tensor.shape[-1]))
    angles = positions.astype(jnp.float32)[:, None] * frequency[None, :]
    cosine = jnp.cos(angles)[:, None, :]
    sine_part = jnp.sin(angles)[:, None, :]
    leading = tensor[..., :half_width]
    trailing = tensor[..., half_width:]
    return jnp.concatenate([leading * cosine - trailing * sine_part, trailing * cosine + leading * sine_part], axis=-1)

def project_heads(normed, wqkv, positions):
    united_rows = jnp.dot(normed, wqkv, preferred_element_type=jnp.float32)
    row_count = united_rows.shape[0]
    queries = rotate(united_rows[:, :H * HD].reshape(row_count, H, HD), positions).astype(jnp.bfloat16)
    new_keys = rotate(united_rows[:, H * HD:(H + KV) * HD].reshape(row_count, KV, HD), positions).astype(jnp.bfloat16)
    new_values = united_rows[:, (H + KV) * HD:].reshape(row_count, KV, HD).astype(jnp.bfloat16)
    return (queries, new_keys, new_values)

def causal_stretch(queries, new_keys, new_values):
    row_count = queries.shape[0]
    group_size = H // KV
    query_heads = jnp.moveaxis(queries.reshape(row_count, KV, group_size, HD), 1, 0)
    key_heads = jnp.moveaxis(new_keys, 1, 0)
    value_heads = jnp.moveaxis(new_values, 1, 0)
    indices = jnp.arange(row_count, dtype=jnp.int32)
    allowed = indices[None, :] <= indices[:, None]

    def one_head(operands):
        query_head, key_head, value_head = operands
        scores = jnp.einsum('qgd,sd->gqs', query_head.astype(jnp.float32), key_head.astype(jnp.float32)) * HD ** (-0.5)
        scores = jnp.where(allowed[None], scores, NEGATIVE)
        highest = lax.optimization_barrier(jnp.max(scores, axis=-1, keepdims=True))
        expanded = jnp.exp(scores - highest)
        weights = (expanded / lax.optimization_barrier(jnp.sum(expanded, axis=-1, keepdims=True))).astype(jnp.bfloat16)
        weights = lax.optimization_barrier(weights)
        return jnp.einsum('gqs,sd->qgd', weights.astype(jnp.float32), value_head.astype(jnp.float32)).astype(jnp.bfloat16)
    attended = lax.map(one_head, (query_heads, key_heads, value_heads))
    return jnp.moveaxis(attended, 0, 1).reshape(row_count, H * HD)

def decode_one(operands):
    queries, self_key, self_value, cache_keys, cache_values, length = operands
    group_size = H // KV
    score_scale = HD ** (-0.5)
    query_heads = queries.reshape(KV, group_size, HD).astype(jnp.float32)
    key_blocks = cache_keys.reshape(N_SHARD, CL_DEV, KV, HD).astype(jnp.float32)
    value_blocks = cache_values.reshape(N_SHARD, CL_DEV, KV, HD).astype(jnp.float32)
    scores = jnp.einsum('kgd,bpkd->bkgp', query_heads, key_blocks) * score_scale
    positions = jnp.arange(N_SHARD * CL_DEV, dtype=jnp.int32).reshape(N_SHARD, 1, 1, CL_DEV)
    live_mask = positions < length
    scores = jnp.where(live_mask, scores, NEGATIVE)
    block_peaks = lax.optimization_barrier(jnp.max(scores, axis=-1))
    expanded = jnp.where(live_mask, jnp.exp(scores - block_peaks[..., None]), 0.0)
    partial_totals = lax.optimization_barrier(jnp.sum(expanded, axis=-1))
    rounded = lax.optimization_barrier(expanded.astype(jnp.bfloat16))
    partial_sums = jnp.einsum('bkgp,bpkd->bkgd', rounded.astype(jnp.float32), value_blocks)
    self_scores = jnp.einsum('kgd,kd->kg', query_heads, self_key.astype(jnp.float32)) * score_scale
    overall = jnp.maximum(lax.optimization_barrier(jnp.max(block_peaks, axis=0)), self_scores)
    rescale = jnp.exp(block_peaks - overall[None])
    own_weight = jnp.exp(self_scores - overall)
    numerator = lax.optimization_barrier(jnp.sum(partial_sums * rescale[..., None], axis=0)) + own_weight[..., None] * self_value.astype(jnp.float32)[:, None, :]
    denominator = lax.optimization_barrier(jnp.sum(partial_totals * rescale, axis=0)) + own_weight
    return (numerator / denominator[..., None]).reshape(H * HD).astype(jnp.bfloat16)

def reference(prefill_x, decode_x, norm_gain, wqkv, wo, k_cache, v_cache, cache_len):
    stretched = prefill_x.reshape(TOKENS // STRETCH, STRETCH, D)

    def one_stretch(inputs):
        normed = normalize(inputs, norm_gain)
        queries, new_keys, new_values = project_heads(normed, wqkv, jnp.arange(STRETCH, dtype=jnp.int32))
        attended = causal_stretch(queries, new_keys, new_values)
        return jnp.dot(attended, wo, preferred_element_type=jnp.float32).astype(jnp.bfloat16)
    prefill_out = lax.map(one_stretch, stretched).reshape(TOKENS, D)
    normed = normalize(decode_x, norm_gain)
    queries, new_keys, new_values = project_heads(normed, wqkv, cache_len)
    attended = lax.map(decode_one, (queries, new_keys, new_values, k_cache, v_cache, cache_len))
    decode_out = jnp.dot(attended, wo, preferred_element_type=jnp.float32).astype(jnp.bfloat16)
    return (prefill_out, decode_out)
```

```python
import jax
import jax.numpy as jnp
from jax import lax
from jax.experimental import pallas as pl
from jax.experimental.pallas import tpu as pltpu
from jax.sharding import PartitionSpec as P

MESH = pl.DeviceIdType.MESH
H, KV, HD = 16, 8, 96
THETA, EPS, NEGATIVE = 100000.0, 1e-05, -1e30
SCALE = HD ** (-0.5)
ORDERS = (("x", "y", "z"), ("y", "z", "x"), ("z", "x", "y"))
N_CHUNK = 3
BF, F32 = jnp.bfloat16, jnp.float32


def coords():
    dp = lax.axis_index("dp"); sh = lax.axis_index("shard")
    core = sh % 2; yhi = (sh // 2) % 2; x = sh // 4
    ylo = dp % 2; z = dp // 2
    return {"x": x, "y": yhi * 2 + ylo, "z": z}, core

def device(c, core):
    return (c["z"] * 2 + c["y"] % 2, c["x"] * 4 + (c["y"] // 2) * 2 + core)

def moved(c, axis, by):
    d = dict(c); d[axis] = (c[axis] + by + 4) % 4
    return d

def block(ref, c, free):
    full = slice(None)
    z = full if "z" in free else c["z"]
    x = full if "x" in free else c["x"]
    ylo = full if "y" in free else c["y"] % 2
    yhi = full if "y" in free else c["y"] // 2
    return ref.at[z, ylo, x, yhi]

class Gather:
    def __init__(self, w, ssem, rsem, dsem_s, dsem_r):
        self.w, self.ssem, self.rsem, self.ds, self.dr = w, ssem, rsem, dsem_s, dsem_r
        self.c, self.core = coords()
        self.sent = []

    def part(self, t, k, core=None):
        core = self.core if core is None else core
        return self.w.at[t * 6 + core * 3 + k]

    def copy(self, t, k, f, s, right, origin):
        order = ORDERS[k]; axis = order[f]
        b = block(self.part(t, k), origin, order[:f])
        if s == 1:
            b = b.at[..., pl.ds(0 if right else 128, 128)]
        i = (((t * 3 + k) * 3 + f) * 2 + s) * 2 + (0 if right else 1)
        return pltpu.make_async_remote_copy(
            src_ref=b, dst_ref=b, send_sem=self.ssem.at[i], recv_sem=self.rsem.at[i],
            device_id=device(moved(self.c, axis, 1 if right else -1), self.core), device_id_type=MESH)

    def send(self, t, f, s):
        for k in range(3):
            axis = ORDERS[k][f]
            for right in (True, False):
                origin = self.c if s == 0 else moved(self.c, axis, -1 if right else 1)
                cp = self.copy(t, k, f, s, right, origin)
                cp.start(); self.sent.append(cp)

    def recv(self, t, f, s):
        for k in range(3):
            axis = ORDERS[k][f]
            for right in (True, False):
                by = (1 + s) * (-1 if right else 1)
                self.copy(t, k, f, s, right, moved(self.c, axis, by)).wait_recv()

    def d2d(self, t, k, j, core):
        order = ORDERS[k]
        b = block(self.part(t, k, core), moved(self.c, order[2], (0, -1, 1, 2)[j]), order[:2])
        i = (t * 3 + k) * 4 + j
        return pltpu.make_async_remote_copy(
            src_ref=b, dst_ref=b, send_sem=self.ds.at[i], recv_sem=self.dr.at[i],
            device_id=device(self.c, 1 - self.core), device_id_type=MESH)

    def give(self, t, js):
        for k in range(3):
            for j in js:
                cp = self.d2d(t, k, j, self.core); cp.start(); self.sent.append(cp)

    def take(self, t):
        for k in range(3):
            for j in range(4):
                self.d2d(t, k, j, 1 - self.core).wait_recv()

    def step(self, t, n):
        if n > 0:
            self.recv(t, (n - 1) // 2, (n - 1) % 2)
        if n < 6:
            self.send(t, n // 2, n % 2)
        if n == 4:
            self.give(t, (0,))
        if n == 5:
            self.give(t, (1, 2))
        if n == 6:
            self.give(t, (3,))

    def finish(self):
        for cp in self.sent:
            cp.wait_send()

def neighbours(c, core):
    out = [device(c, 1 - core)]
    for axis in ("x", "y", "z"):
        for by in (1, -1):
            out.append(device(moved(c, axis, by), core))
    return out + [partner(c, core, 1), partner(c, core, 3)]

def barrier(c, core):
    sem = pltpu.get_barrier_semaphore()
    for d in neighbours(c, core):
        pl.semaphore_signal(sem, inc=1, device_id=d, device_id_type=MESH)
    pl.semaphore_wait(sem, 9)

def merge(dst, own, other, core):
    a = own.astype(jnp.float32); b = other.astype(jnp.float32)
    first = jnp.where(core == 0, a, b); second = jnp.where(core == 0, b, a)
    return jnp.concatenate([first, second], axis=-2).astype(dst)

class GainRing:
    def __init__(self, g, ssem, rsem):
        self.g, self.ssem, self.rsem = g, ssem, rsem
        self.c, self.core = coords()
        self.sent = []

    def copy(self, f, s, right, origin):
        order = ORDERS[0]
        b = block(self.g, origin, order[:f])
        i = (f * 2 + s) * 2 + (0 if right else 1)
        return pltpu.make_async_remote_copy(
            src_ref=b, dst_ref=b, send_sem=self.ssem.at[i], recv_sem=self.rsem.at[i],
            device_id=device(moved(self.c, order[f], 1 if right else -1), self.core), device_id_type=MESH)

    def step(self, n):
        axes = ORDERS[0]
        if n > 0:
            f, s = (n - 1) // 2, (n - 1) % 2
            for right in (True, False) if s == 0 else (True,):
                self.copy(f, s, right, moved(self.c, axes[f], (1 + s) * (-1 if right else 1))).wait_recv()
        if n < 6:
            f, s = n // 2, n % 2
            for right in (True, False) if s == 0 else (True,):
                cp = self.copy(f, s, right, self.c if s == 0 else moved(self.c, axes[f], -1))
                cp.start()
                self.sent.append(cp)

    def finish(self):
        for cp in self.sent:
            cp.wait_send()


def gain_row(g):
    tiles = g[...].astype(F32).reshape(64, 8, 128)
    values = jnp.sum(tiles, axis=1).astype(BF)
    column = lax.broadcasted_iota(jnp.int32, (64, 1536), 1)
    chip = lax.broadcasted_iota(jnp.int32, (64, 1536), 0) * 24
    mine = jnp.where((column >= chip) & (column < chip + 24), 1.0, 0.0).astype(BF)
    spread = lax.dot_general(values, mine, (((0,), (0,)), ((), ())), preferred_element_type=F32)
    n = lax.broadcasted_iota(jnp.int32, (128, 1536), 1).astype(F32)
    within = n - 24.0 * jnp.floor((n + 0.5) * (1.0 / 24.0))
    j = lax.broadcasted_iota(jnp.int32, (128, 1536), 0).astype(F32)
    return jnp.sum(jnp.where(within == j, spread, 0.0), axis=0, keepdims=True)


def normalize(xb, nb, gain):
    def rows(start, size):
        wide = xb[pl.ds(start, size), :].astype(F32)
        factor = lax.rsqrt(jnp.mean(wide * wide, axis=-1, keepdims=True) + EPS)
        nb[pl.ds(start, size), :] = (wide * factor * gain).astype(BF)

    @pl.loop(0, 12)
    def _(i):
        rows(pl.multiple_of(i * 64, 64), 64)

    rows(768, 16)


def project(nb, w, u, t, lo, hi):
    @pl.loop(lo, hi)
    def _(j):
        rhs = w[t * 6 + j].reshape(1536, 256)
        u[:, pl.ds(pl.multiple_of(j * 256, 256), 256)] = jnp.dot(nb[...], rhs, preferred_element_type=F32)


def heads(u, cos, sin, qh, kh, vh, t):
    def turned(lo, half, r, c, s):
        a, b = u[r, lo : lo + half], u[r, lo + half : lo + 2 * half]
        return (a * c - b * s).astype(BF), (b * c + a * s).astype(BF)

    @pl.loop(0, 7)
    def _(i):
        r = pl.ds(pl.multiple_of(i * 112, 16), 112)
        c, s = cos[r, :], sin[r, :]
        a, b = turned(0, 384, r, c, s)
        for h in range(8):
            qh[8 * t + h, r, :] = jnp.concatenate([a[:, 48 * h : 48 * h + 48], b[:, 48 * h : 48 * h + 48]], axis=1)
        a, b = turned(768, 192, r, c[:, :192], s[:, :192])
        for h in range(4):
            kh[4 * t + h, r, :] = jnp.concatenate([a[:, 48 * h : 48 * h + 48], b[:, 48 * h : 48 * h + 48]], axis=1)
        for h in range(4):
            vh[4 * t + h, r, :] = u[r, 1152 + 96 * h : 1248 + 96 * h].astype(BF)


def attend(qh, kh, vh, attn, g):
    for i in range(3):
        lo, n = 256 * i, 256 * (i + 1)
        q = jnp.concatenate([qh[2 * g, lo:n, :], qh[2 * g + 1, lo:n, :]], axis=0)
        s = lax.dot_general(q, kh[g, 0:n, :], (((1,), (1,)), ((), ())), preferred_element_type=F32)
        row = lax.broadcasted_iota(jnp.int32, (512, 256), 0) & 255
        column = lax.broadcasted_iota(jnp.int32, (512, 256), 1)
        last = jnp.where(column <= row, s[:, lo:n], NEGATIVE)
        s = jnp.concatenate([s[:, :lo], last], axis=1) if i else last
        s = s * SCALE
        e = jnp.exp(s - jnp.max(s, axis=-1, keepdims=True))
        total = jnp.sum(e, axis=-1, keepdims=True)
        o = jnp.dot(e.astype(BF), vh[g, 0:n, :], preferred_element_type=F32)
        o = (o / total).astype(BF)
        attn[lo:n, 192 * g : 192 * g + 192] = jnp.concatenate([o[:256], o[256:]], axis=1)


def decode_block(qh, kc, vc, clen, pk, wide):
    q = qh[:, 768:784, :].astype(F32)
    lane = lax.broadcasted_iota(jnp.int32, (16, 768), 1)
    first = (lax.broadcasted_iota(jnp.int32, (16, 768), 0) // 2) * 96
    mine = (lane >= first) & (lane < first + 96)
    at = lax.axis_index("shard") * 512 + lax.broadcasted_iota(jnp.int32, (16, 512), 1)
    for r in range(8):
        one = q[:, r, :]
        spread = jnp.concatenate([one] * 8, axis=1)
        qw = jnp.where(mine, spread, 0.0).astype(BF)
        s = lax.dot_general(qw, kc[r], (((1,), (1,)), ((), ())), preferred_element_type=F32) * SCALE
        live = at < clen[r]
        s = jnp.where(live, s, NEGATIVE)
        peak = jnp.max(s, axis=-1, keepdims=True)
        e = jnp.where(live, jnp.exp(s - peak), 0.0)
        total = jnp.sum(e, axis=-1, keepdims=True)
        every = jnp.where(mine, jnp.dot(e.astype(BF), vc[r], preferred_element_type=F32), 0.0)
        acc = every[:, 0:96]
        for g in range(1, 8):
            acc = acc + every[:, 96 * g : 96 * g + 96]
        pk[:, r, :] = jnp.concatenate(
            [acc, jnp.broadcast_to(peak, (16, 16)), jnp.broadcast_to(total, (16, 16))], axis=1)


class Combine:
    def __init__(self, pk, rv, ssem, rsem):
        self.pk, self.rv, self.ssem, self.rsem = pk, rv, ssem, rsem
        self.sent = []

    def copy(self, j):
        c, core = coords()
        return pltpu.make_async_remote_copy(
            src_ref=self.pk.at[j], dst_ref=self.rv.at[j], send_sem=self.ssem.at[j], recv_sem=self.rsem.at[j],
            device_id=partner(c, core, j), device_id_type=MESH)

    def send(self, j):
        cp = self.copy(j)
        cp.start()
        self.sent.append(cp)

    def add(self, j):
        self.copy(j).wait_recv()
        a, b = self.pk[j], self.rv[j]
        pa, pb = a[:, :, 96:97], b[:, :, 96:97]
        top = jnp.maximum(pa, pb)
        both = a * jnp.exp(pa - top) + b * jnp.exp(pb - top)
        lane = lax.broadcasted_iota(jnp.int32, both.shape, 2)
        self.pk[j + 1] = jnp.where((lane >= 96) & (lane < 112), top, both)

    def finish(self):
        for cp in self.sent:
            cp.wait_send()


def partner(c, core, j):
    if j == 0:
        return device(c, 1 - core)
    if j == 1:
        return device(moved(c, "y", 2), core)
    if j == 2:
        return device({**c, "x": c["x"] + 1 - 2 * (c["x"] % 2)}, core)
    return device(moved(c, "x", 2), core)


def decode_mix(pk, qh, kh, vh, attn):
    a = pk[4]
    acc, peak, total = a[:, :, 0:96], a[:, :, 96:97], a[:, :, 112:113]

    def pairs(ref):
        v = ref[:, 768:784, :].astype(F32)[:, 0:8, :]
        return jnp.broadcast_to(v[:, None], (8, 2, 8, 96)).reshape(16, 8, 96)

    q = qh[:, 768:784, :].astype(F32)[:, 0:8, :]
    own = jnp.sum(q * pairs(kh), axis=-1, keepdims=True) * SCALE
    top = jnp.maximum(peak, own)
    old, new = jnp.exp(peak - top), jnp.exp(own - top)
    mix = (acc * old + new * pairs(vh)) / (total * old + new)
    zero = jnp.zeros((8, 96), F32)
    for h in range(16):
        attn[768:784, 96 * h : 96 * h + 96] = jnp.concatenate([mix[h], zero], axis=0).astype(BF)


def kernel(slab_ref, gain_ref, x_ref, dx_ref, cos, sin, k_ref, v_ref, clen, out_ref, dout_ref,
           own, other, gown, gother, w, g, xb, nb, u, qh, kh, vh, attn, kc, vc, o, pk, rv,
           ssem, rsem, ds, dr, ps, pr, gs, gr, cs, cr, lsem, osem):
    c, core = coords()
    loads = [pltpu.make_async_copy(s, d, lsem.at[i]) for i, (s, d) in enumerate((
        (slab_ref, own), (gain_ref, gown), (x_ref, xb.at[pl.ds(0, 768)]), (dx_ref, xb.at[pl.ds(768, 16)]),
        (k_ref, kc), (v_ref, vc)))]
    for cp in loads[:2]:
        cp.start()
    barrier(c, core)
    for cp in loads[:2]:
        cp.wait()
    pre = [pltpu.make_async_remote_copy(
        src_ref=s, dst_ref=d, send_sem=ps.at[i], recv_sem=pr.at[i],
        device_id=device(c, 1 - core), device_id_type=MESH)
        for i, (s, d) in enumerate(((own.at[1 - core], other), (gown, gother)))]
    for cp in pre:
        cp.start()
    for cp in loads[2:]:
        cp.start()
    for cp in pre:
        cp.wait()
    for i in range(3 * N_CHUNK):
        t, k = i // 3, i % 3
        w[t * 6 + core * 3 + k, c["z"], c["y"] % 2, c["x"], c["y"] // 2] = merge(BF, own[core, i], other[i], core)
    g[c["z"], c["y"] % 2, c["x"], c["y"] // 2] = (gown[...].astype(F32) + gother[...].astype(F32)).astype(BF)
    G = Gather(w, ssem, rsem, ds, dr)
    R = GainRing(g, gs, gr)
    D = Combine(pk, rv, cs, cr)

    for tick in range(5):
        R.step(tick)
        for t in range(N_CHUNK):
            if 0 <= tick - LAG * t <= 6:
                G.step(t, tick - LAG * t)
    R.step(5)
    R.step(6)
    for cp in loads[2:4]:
        cp.wait()
    normalize(xb, nb, gain_row(g))
    G.step(0, 5)
    G.step(1, 3)
    G.step(2, 1)
    G.step(0, 6)
    G.step(1, 4)
    G.step(2, 2)
    G.take(0)
    project(nb, w, u, 0, 0, 3)
    G.step(2, 3)
    project(nb, w, u, 0, 3, 6)
    G.step(1, 5)
    heads(u, cos, sin, qh, kh, vh, 0)
    G.step(1, 6)
    G.step(2, 4)
    attend(qh, kh, vh, attn, 0)
    attend(qh, kh, vh, attn, 1)
    G.step(2, 5)
    attend(qh, kh, vh, attn, 2)
    attend(qh, kh, vh, attn, 3)
    G.step(2, 6)
    G.take(1)
    project(nb, w, u, 1, 0, 6)
    heads(u, cos, sin, qh, kh, vh, 1)
    for cp in loads[4:]:
        cp.wait()
    decode_block(qh, kc, vc, clen, pk.at[0], None)
    for j in range(4):
        D.send(j)
        attend(qh, kh, vh, attn, 4 + j)
        D.add(j)
    decode_mix(pk, qh, kh, vh, attn)
    G.take(2)

    @pl.loop(0, 6)
    def _(j):
        rhs = w[12 + j].reshape(1536, 256)
        o[:, pl.ds(pl.multiple_of(j * 256, 256), 256)] = jnp.dot(
            attn[...], rhs, preferred_element_type=F32).astype(BF)

    outs = [pltpu.make_async_copy(o.at[pl.ds(0, 768)], out_ref, osem.at[0]),
            pltpu.make_async_copy(o.at[pl.ds(768, 16)], dout_ref, osem.at[1])]
    for cp in outs:
        cp.start()
    G.finish()
    R.finish()
    D.finish()
    for cp in outs:
        cp.wait()


LAG = 2


def per_device(prefill_x, decode_x, norm_gain, wqkv, wo, k_cache, v_cache, cache_len):
    q = wqkv[:, :1536].reshape(12, 2, 8, 2, 48).transpose(1, 0, 3, 2, 4).reshape(2, 12, 768)
    k = wqkv[:, 1536:2304].reshape(12, 2, 4, 2, 48).transpose(1, 0, 3, 2, 4).reshape(2, 12, 384)
    v = wqkv[:, 2304:].reshape(12, 2, 384).transpose(1, 0, 2)
    chunks = jnp.concatenate([jnp.concatenate([q, k, v], axis=2), wo[None]], axis=0)
    slab = chunks.reshape(3, 12, 2, 3, 256).transpose(2, 0, 3, 1, 4).reshape(2, 9, 12, 256)
    core = lax.axis_index("shard") % 2
    row = jnp.concatenate([jnp.where(core == 0, norm_gain, 0), jnp.where(core == 1, norm_gain, 0)])
    gain_tile = jnp.pad(row[None], ((0, 7), (0, 104)))
    frequency = jnp.power(THETA, -jnp.arange(48, dtype=F32) * (2.0 / HD))
    positions = jnp.concatenate([jnp.arange(768, dtype=jnp.int32), cache_len, jnp.zeros((8,), jnp.int32)])
    angles = positions.astype(F32)[:, None] * frequency[None, :]
    cos = jnp.tile(jnp.cos(angles), (1, 8))
    sin = jnp.tile(jnp.sin(angles), (1, 8))
    dx = jnp.concatenate([decode_x, jnp.zeros((8, 1536), BF)], axis=0)
    hbm, vmem = pl.BlockSpec(memory_space=pl.ANY), pl.BlockSpec(memory_space=pltpu.VMEM)
    n = N_CHUNK
    dma = pltpu.SemaphoreType.DMA
    out, dout = pl.pallas_call(
        kernel,
        out_shape=(jax.ShapeDtypeStruct((768, 1536), BF), jax.ShapeDtypeStruct((16, 1536), BF)),
        in_specs=[hbm, hbm, hbm, hbm, vmem, vmem, hbm, hbm, pl.BlockSpec(memory_space=pltpu.SMEM)],
        out_specs=(hbm, hbm),
        scratch_shapes=[
            pltpu.VMEM((2, 3 * n, 12, 256), BF), pltpu.VMEM((3 * n, 12, 256), BF),
            pltpu.VMEM((8, 128), BF), pltpu.VMEM((8, 128), BF),
            pltpu.VMEM((6 * n, 4, 2, 4, 2, 24, 256), BF), pltpu.VMEM((4, 2, 4, 2, 8, 128), BF),
            pltpu.VMEM((784, 1536), BF), pltpu.VMEM((784, 1536), BF), pltpu.VMEM((784, 1536), F32),
            pltpu.VMEM((16, 784, 96), BF), pltpu.VMEM((8, 784, 96), BF), pltpu.VMEM((8, 784, 96), BF),
            pltpu.VMEM((784, 1536), BF), pltpu.VMEM((8, 512, 768), BF), pltpu.VMEM((8, 512, 768), BF),
            pltpu.VMEM((784, 1536), BF), pltpu.VMEM((5, 16, 8, 128), F32), pltpu.VMEM((4, 16, 8, 128), F32),
            dma((36 * n,)), dma((36 * n,)), dma((12 * n,)), dma((12 * n,)), dma((2,)), dma((2,)),
            dma((12,)), dma((12,)), dma((4,)), dma((4,)), dma((6,)), dma((2,)),
        ],
        compiler_params=pltpu.CompilerParams(
            collective_id=0, has_side_effects=True, vmem_limit_bytes=67043328),
        name="sublayer",
    )(slab, gain_tile, prefill_x, dx, cos, sin, k_cache, v_cache, cache_len)
    return out, dout[:8]


def solution(mesh):
    rows = P(("dp", "shard"), None)
    in_specs = (rows, P("dp", None), P(("dp", "shard")), rows, rows,
                P("dp", "shard", None), P("dp", "shard", None), P("dp"))
    return jax.shard_map(per_device, mesh=mesh, in_specs=in_specs,
                         out_specs=(rows, P("dp", None)), check_vma=False)
```

```python
import jax
import jax.numpy as jnp
import numpy as np
from jax import lax
from jax.experimental import pallas as pl
from jax.experimental.pallas import tpu as pltpu
from jax.sharding import PartitionSpec as P

MESH = pl.DeviceIdType.MESH
H, KV, HD = 16, 8, 96
THETA, EPS, NEGATIVE = 100000.0, 1e-05, -1e30
SCALE = HD ** (-0.5)
ORDERS = (("x", "y", "z"), ("y", "z", "x"), ("z", "x", "y"))
N_CHUNK = 3
BF, F32 = jnp.bfloat16, jnp.float32


def coords():
    dp = lax.axis_index("dp"); sh = lax.axis_index("shard")
    core = sh % 2; yhi = (sh // 2) % 2; x = sh // 4
    ylo = dp % 2; z = dp // 2
    return {"x": x, "y": yhi * 2 + ylo, "z": z}, core

def device(c, core):
    return (c["z"] * 2 + c["y"] % 2, c["x"] * 4 + (c["y"] // 2) * 2 + core)

def moved(c, axis, by):
    d = dict(c); d[axis] = (c[axis] + by + 4) % 4
    return d

def block(ref, c, free):
    full = slice(None)
    z = full if "z" in free else c["z"]
    x = full if "x" in free else c["x"]
    ylo = full if "y" in free else c["y"] % 2
    yhi = full if "y" in free else c["y"] // 2
    return ref.at[z, ylo, x, yhi]

class Gather:
    def __init__(self, w, ssem, rsem, dsem_s, dsem_r):
        self.w, self.ssem, self.rsem, self.ds, self.dr = w, ssem, rsem, dsem_s, dsem_r
        self.c, self.core = coords()
        self.sent = []

    def part(self, t, k, core=None):
        core = self.core if core is None else core
        return self.w.at[t * 6 + core * 3 + k]

    def copy(self, t, k, f, s, right, origin):
        order = ORDERS[k]; axis = order[f]
        b = block(self.part(t, k), origin, order[:f])
        if s == 1:
            b = b.at[..., pl.ds(0 if right else 128, 128)]
        i = (((t * 3 + k) * 3 + f) * 2 + s) * 2 + (0 if right else 1)
        return pltpu.make_async_remote_copy(
            src_ref=b, dst_ref=b, send_sem=self.ssem.at[i], recv_sem=self.rsem.at[i],
            device_id=device(moved(self.c, axis, 1 if right else -1), self.core), device_id_type=MESH)

    def send(self, t, f, s):
        for k in range(3):
            axis = ORDERS[k][f]
            for right in (True, False):
                origin = self.c if s == 0 else moved(self.c, axis, -1 if right else 1)
                cp = self.copy(t, k, f, s, right, origin)
                cp.start(); self.sent.append(cp)

    def recv(self, t, f, s):
        for k in range(3):
            axis = ORDERS[k][f]
            for right in (True, False):
                by = (1 + s) * (-1 if right else 1)
                self.copy(t, k, f, s, right, moved(self.c, axis, by)).wait_recv()

    def d2d(self, t, k, j, core):
        order = ORDERS[k]
        b = block(self.part(t, k, core), moved(self.c, order[2], (0, -1, 1, 2)[j]), order[:2])
        i = (t * 3 + k) * 4 + j
        return pltpu.make_async_remote_copy(
            src_ref=b, dst_ref=b, send_sem=self.ds.at[i], recv_sem=self.dr.at[i],
            device_id=device(self.c, 1 - self.core), device_id_type=MESH)

    def give(self, t, js):
        for k in range(3):
            for j in js:
                cp = self.d2d(t, k, j, self.core); cp.start(); self.sent.append(cp)

    def take(self, t):
        for k in range(3):
            for j in range(4):
                self.d2d(t, k, j, 1 - self.core).wait_recv()

    def step(self, t, n):
        if n > 0:
            self.recv(t, (n - 1) // 2, (n - 1) % 2)
        if n < 6:
            self.send(t, n // 2, n % 2)
        if n == 4:
            self.give(t, (0,))
        if n == 5:
            self.give(t, (1, 2))
        if n == 6:
            self.give(t, (3,))

    def finish(self):
        for cp in self.sent:
            cp.wait_send()

def neighbours(c, core):
    out = [device(c, 1 - core)]
    for axis in ("x", "y", "z"):
        for by in (1, -1):
            out.append(device(moved(c, axis, by), core))
    return out + [partner(c, core, 1), partner(c, core, 3)]

def barrier(c, core):
    sem = pltpu.get_barrier_semaphore()
    for d in neighbours(c, core):
        pl.semaphore_signal(sem, inc=1, device_id=d, device_id_type=MESH)
    pl.semaphore_wait(sem, 9)

def both_rows(own, other, core):
    a, b = own[...].astype(F32), other[...].astype(F32)
    return jnp.concatenate([jnp.where(core == 0, a, b), jnp.where(core == 0, b, a)], axis=0)


def merge(t, own_q, other_q, own_o, other_o, w, c, core):
    if t == 2:
        cols = both_rows(own_o, other_o, core)
    else:
        a = both_rows(own_q, other_q, core)
        starts = [96 * (8 * t + h) + 48 * half for half in range(2) for h in range(8)]
        starts += [1536 + 96 * (4 * t + h) + 48 * half for half in range(2) for h in range(4)]
        v = 2304 + 384 * t
        cols = jnp.concatenate([a[:, n : n + 48] for n in starts] + [a[:, v : v + 384]], axis=1)
    for k in range(3):
        part = jnp.where(core == 0, cols[:, 256 * k : 256 * k + 256], cols[:, 768 + 256 * k : 1024 + 256 * k])
        w[t * 6 + core * 3 + k, c["z"], c["y"] % 2, c["x"], c["y"] // 2] = part.astype(BF)


def gain_tile(gain, core):
    g = gain[...].astype(F32)
    zero = jnp.zeros((1, 116), F32)
    row = jnp.where(core == 0, jnp.concatenate([g, zero], axis=1),
                    jnp.concatenate([zero[:, :12], g, zero[:, :104]], axis=1))
    first = lax.broadcasted_iota(jnp.int32, (8, 128), 0) == 0
    return jnp.where(first, jnp.broadcast_to(row, (8, 128)), 0.0).astype(BF)


def angles(freq, clen, cos, sin):
    def put(start, size, at):
        a = at.astype(F32) * freq[...]
        rows = pl.ds(start, size)
        cos[rows, :] = jnp.concatenate([jnp.cos(a)[:, :48]] * 8, axis=1)
        sin[rows, :] = jnp.concatenate([jnp.sin(a)[:, :48]] * 8, axis=1)

    @pl.loop(0, 16)
    def _(i):
        put(pl.multiple_of(i * 48, 16), 48, lax.broadcasted_iota(jnp.int32, (48, 128), 0) + i * 48)

    row = lax.broadcasted_iota(jnp.int32, (16, 128), 0)
    at = jnp.zeros((16, 128), jnp.int32)
    for r in range(8):
        at = jnp.where(row == r, clen[r], at)
    put(768, 16, at)


class GainRing:
    def __init__(self, g, ssem, rsem):
        self.g, self.ssem, self.rsem = g, ssem, rsem
        self.c, self.core = coords()
        self.sent = []

    def copy(self, f, s, right, origin):
        order = ORDERS[0]
        b = block(self.g, origin, order[:f])
        i = (f * 2 + s) * 2 + (0 if right else 1)
        return pltpu.make_async_remote_copy(
            src_ref=b, dst_ref=b, send_sem=self.ssem.at[i], recv_sem=self.rsem.at[i],
            device_id=device(moved(self.c, order[f], 1 if right else -1), self.core), device_id_type=MESH)

    def step(self, n):
        axes = ORDERS[0]
        if n > 0:
            f, s = (n - 1) // 2, (n - 1) % 2
            for right in (True, False) if s == 0 else (True,):
                self.copy(f, s, right, moved(self.c, axes[f], (1 + s) * (-1 if right else 1))).wait_recv()
        if n < 6:
            f, s = n // 2, n % 2
            for right in (True, False) if s == 0 else (True,):
                cp = self.copy(f, s, right, self.c if s == 0 else moved(self.c, axes[f], -1))
                cp.start()
                self.sent.append(cp)

    def finish(self):
        for cp in self.sent:
            cp.wait_send()


def gain_row(g):
    tiles = g[...].astype(F32).reshape(64, 8, 128)
    values = jnp.sum(tiles, axis=1).astype(BF)
    column = lax.broadcasted_iota(jnp.int32, (64, 1536), 1)
    chip = lax.broadcasted_iota(jnp.int32, (64, 1536), 0) * 24
    mine = jnp.where((column >= chip) & (column < chip + 24), 1.0, 0.0).astype(BF)
    spread = lax.dot_general(values, mine, (((0,), (0,)), ((), ())), preferred_element_type=F32)
    n = lax.broadcasted_iota(jnp.int32, (128, 1536), 1).astype(F32)
    within = n - 24.0 * jnp.floor((n + 0.5) * (1.0 / 24.0))
    j = lax.broadcasted_iota(jnp.int32, (128, 1536), 0).astype(F32)
    return jnp.sum(jnp.where(within == j, spread, 0.0), axis=0, keepdims=True)


def normalize(xb, nb, gain):
    def scaled(start, size):
        wide = xb[pl.ds(start, size), :].astype(F32)
        factor = lax.rsqrt(jnp.mean(wide * wide, axis=-1, keepdims=True) + EPS)
        return wide * factor * gain

    @pl.loop(0, 12)
    def _(i):
        start = pl.multiple_of(i * 64, 64)
        nb[pl.ds(start, 64), :] = scaled(start, 64).astype(BF)

    nb[768:784, :] = jnp.concatenate([scaled(768, 8), jnp.zeros((8, 1536), F32)], axis=0).astype(BF)


def project(nb, w, u, t, lo, hi):
    @pl.loop(lo, hi)
    def _(j):
        rhs = w[t * 6 + j].reshape(1536, 256)
        u[:, pl.ds(pl.multiple_of(j * 256, 256), 256)] = jnp.dot(nb[...], rhs, preferred_element_type=F32)


def heads(u, cos, sin, qh, kh, vh, t):
    def turned(lo, half, r, c, s):
        a, b = u[r, lo : lo + half], u[r, lo + half : lo + 2 * half]
        return (a * c - b * s).astype(BF), (b * c + a * s).astype(BF)

    @pl.loop(0, 7)
    def _(i):
        r = pl.ds(pl.multiple_of(i * 112, 16), 112)
        c, s = cos[r, :], sin[r, :]
        a, b = turned(0, 384, r, c, s)
        for h in range(8):
            qh[8 * t + h, r, :] = jnp.concatenate([a[:, 48 * h : 48 * h + 48], b[:, 48 * h : 48 * h + 48]], axis=1)
        a, b = turned(768, 192, r, c[:, :192], s[:, :192])
        for h in range(4):
            kh[4 * t + h, r, :] = jnp.concatenate([a[:, 48 * h : 48 * h + 48], b[:, 48 * h : 48 * h + 48]], axis=1)
        for h in range(4):
            vh[4 * t + h, r, :] = u[r, 1152 + 96 * h : 1248 + 96 * h].astype(BF)


def attend(qh, kh, vh, attn, g):
    for i in range(3):
        lo, n = 256 * i, 256 * (i + 1)
        q = jnp.concatenate([qh[2 * g, lo:n, :], qh[2 * g + 1, lo:n, :]], axis=0)
        s = lax.dot_general(q, kh[g, 0:n, :], (((1,), (1,)), ((), ())), preferred_element_type=F32)
        row = lax.broadcasted_iota(jnp.int32, (512, 256), 0) & 255
        column = lax.broadcasted_iota(jnp.int32, (512, 256), 1)
        last = jnp.where(column <= row, s[:, lo:n], NEGATIVE)
        s = jnp.concatenate([s[:, :lo], last], axis=1) if i else last
        s = s * SCALE
        e = jnp.exp(s - jnp.max(s, axis=-1, keepdims=True))
        total = jnp.sum(e, axis=-1, keepdims=True)
        o = jnp.dot(e.astype(BF), vh[g, 0:n, :], preferred_element_type=F32)
        o = (o / total).astype(BF)
        attn[lo:n, 192 * g : 192 * g + 192] = jnp.concatenate([o[:256], o[256:]], axis=1)


def decode_block(qh, kc, vc, clen, pk, wide):
    q = qh[:, 768:784, :].astype(F32)
    lane = lax.broadcasted_iota(jnp.int32, (16, 768), 1)
    first = (lax.broadcasted_iota(jnp.int32, (16, 768), 0) // 2) * 96
    mine = (lane >= first) & (lane < first + 96)
    at = lax.axis_index("shard") * 512 + lax.broadcasted_iota(jnp.int32, (16, 512), 1)
    for r in range(8):
        one = q[:, r, :]
        spread = jnp.concatenate([one] * 8, axis=1)
        qw = jnp.where(mine, spread, 0.0).astype(BF)
        s = lax.dot_general(qw, kc[r], (((1,), (1,)), ((), ())), preferred_element_type=F32) * SCALE
        live = at < clen[r]
        s = jnp.where(live, s, NEGATIVE)
        peak = jnp.max(s, axis=-1, keepdims=True)
        e = jnp.where(live, jnp.exp(s - peak), 0.0)
        total = jnp.sum(e, axis=-1, keepdims=True)
        every = jnp.where(mine, jnp.dot(e.astype(BF), vc[r], preferred_element_type=F32), 0.0)
        acc = every[:, 0:96]
        for g in range(1, 8):
            acc = acc + every[:, 96 * g : 96 * g + 96]
        pk[:, r, :] = jnp.concatenate(
            [acc, jnp.broadcast_to(peak, (16, 16)), jnp.broadcast_to(total, (16, 16))], axis=1)


class Combine:
    def __init__(self, pk, rv, ssem, rsem):
        self.pk, self.rv, self.ssem, self.rsem = pk, rv, ssem, rsem
        self.sent = []

    def copy(self, j):
        c, core = coords()
        return pltpu.make_async_remote_copy(
            src_ref=self.pk.at[j], dst_ref=self.rv.at[j], send_sem=self.ssem.at[j], recv_sem=self.rsem.at[j],
            device_id=partner(c, core, j), device_id_type=MESH)

    def send(self, j):
        cp = self.copy(j)
        cp.start()
        self.sent.append(cp)

    def add(self, j):
        self.copy(j).wait_recv()
        a, b = self.pk[j], self.rv[j]
        pa, pb = a[:, :, 96:97], b[:, :, 96:97]
        top = jnp.maximum(pa, pb)
        both = a * jnp.exp(pa - top) + b * jnp.exp(pb - top)
        lane = lax.broadcasted_iota(jnp.int32, both.shape, 2)
        self.pk[j + 1] = jnp.where((lane >= 96) & (lane < 112), top, both)

    def finish(self):
        for cp in self.sent:
            cp.wait_send()


def partner(c, core, j):
    if j == 0:
        return device(c, 1 - core)
    if j == 1:
        return device(moved(c, "y", 2), core)
    if j == 2:
        return device({**c, "x": c["x"] + 1 - 2 * (c["x"] % 2)}, core)
    return device(moved(c, "x", 2), core)


def decode_mix(pk, qh, kh, vh, attn):
    a = pk[4]
    acc, peak, total = a[:, :, 0:96], a[:, :, 96:97], a[:, :, 112:113]

    def pairs(ref):
        v = ref[:, 768:784, :].astype(F32)[:, 0:8, :]
        return jnp.broadcast_to(v[:, None], (8, 2, 8, 96)).reshape(16, 8, 96)

    q = qh[:, 768:784, :].astype(F32)[:, 0:8, :]
    own = jnp.sum(q * pairs(kh), axis=-1, keepdims=True) * SCALE
    top = jnp.maximum(peak, own)
    old, new = jnp.exp(peak - top), jnp.exp(own - top)
    mix = (acc * old + new * pairs(vh)) / (total * old + new)
    zero = jnp.zeros((8, 96), F32)
    for h in range(16):
        attn[768:784, 96 * h : 96 * h + 96] = jnp.concatenate([mix[h], zero], axis=0).astype(BF)


def kernel(wq_ref, wo_ref, gain_ref, x_ref, dx_ref, freq, k_ref, v_ref, clen, out_ref, dout_ref,
           own_q, own_o, other_q, other_o, gown, gother, w, g, xb, nb, u, cos, sin, qh, kh, vh, attn, kc, vc, o, pk, rv,
           ssem, rsem, ds, dr, ps, pr, gs, gr, cs, cr, lsem, osem):
    c, core = coords()
    loads = [pltpu.make_async_copy(s, d, lsem.at[i]) for i, (s, d) in enumerate((
        (wq_ref, own_q), (wo_ref, own_o), (x_ref, xb.at[pl.ds(0, 768)]), (dx_ref, xb.at[pl.ds(768, 8)]),
        (k_ref, kc), (v_ref, vc)))]
    for cp in loads[:2]:
        cp.start()
    gown[...] = gain_tile(gain_ref, core)
    barrier(c, core)
    pre = [pltpu.make_async_remote_copy(
        src_ref=s, dst_ref=d, send_sem=ps.at[i], recv_sem=pr.at[i],
        device_id=device(c, 1 - core), device_id_type=MESH)
        for i, (s, d) in enumerate(((wq_ref, other_q), (wo_ref, other_o), (gown, gother)))]
    for cp in pre:
        cp.start()
    for cp in loads[2:]:
        cp.start()
    for cp in loads[:2]:
        cp.wait()
    for cp in pre:
        cp.wait()
    g[c["z"], c["y"] % 2, c["x"], c["y"] // 2] = (gown[...].astype(F32) + gother[...].astype(F32)).astype(BF)
    G = Gather(w, ssem, rsem, ds, dr)
    R = GainRing(g, gs, gr)
    D = Combine(pk, rv, cs, cr)

    for tick in range(5):
        R.step(tick)
        for t in range(N_CHUNK):
            if tick == LAG * t:
                merge(t, own_q, other_q, own_o, other_o, w, c, core)
            if 0 <= tick - LAG * t <= 6:
                G.step(t, tick - LAG * t)
    R.step(5)
    angles(freq, clen, cos, sin)
    R.step(6)
    for cp in loads[2:4]:
        cp.wait()
    normalize(xb, nb, gain_row(g))
    G.step(0, 5)
    G.step(1, 3)
    G.step(2, 1)
    G.step(0, 6)
    G.step(1, 4)
    G.step(2, 2)
    G.take(0)
    project(nb, w, u, 0, 0, 3)
    G.step(2, 3)
    project(nb, w, u, 0, 3, 6)
    G.step(1, 5)
    heads(u, cos, sin, qh, kh, vh, 0)
    G.step(1, 6)
    G.step(2, 4)
    attend(qh, kh, vh, attn, 0)
    attend(qh, kh, vh, attn, 1)
    G.step(2, 5)
    attend(qh, kh, vh, attn, 2)
    attend(qh, kh, vh, attn, 3)
    G.step(2, 6)
    G.take(1)
    project(nb, w, u, 1, 0, 6)
    heads(u, cos, sin, qh, kh, vh, 1)
    for cp in loads[4:]:
        cp.wait()
    decode_block(qh, kc, vc, clen, pk.at[0], None)
    for j in range(4):
        D.send(j)
        attend(qh, kh, vh, attn, 4 + j)
        D.add(j)
    decode_mix(pk, qh, kh, vh, attn)
    G.take(2)

    def leaving(j):
        cols = pl.ds(pl.multiple_of(j * 256, 256), 256)
        return pltpu.make_async_copy(o.at[pl.ds(0, 768), cols], out_ref.at[:, cols], osem.at[j])

    @pl.loop(0, 6)
    def _(j):
        rhs = w[12 + j].reshape(1536, 256)
        o[:, pl.ds(pl.multiple_of(j * 256, 256), 256)] = jnp.dot(
            attn[...], rhs, preferred_element_type=F32).astype(BF)
        leaving(j).start()

    outs = [leaving(j) for j in range(6)]
    outs.append(pltpu.make_async_copy(o.at[pl.ds(768, 8)], dout_ref, osem.at[6]))
    outs[6].start()
    G.finish()
    R.finish()
    D.finish()
    for cp in outs:
        cp.wait()


LAG = 2


def per_device(prefill_x, decode_x, norm_gain, wqkv, wo, k_cache, v_cache, cache_len):
    freq = np.power(np.float32(THETA), -np.arange(48, dtype=np.float32) * np.float32(2.0 / HD))
    freq = jnp.asarray(np.pad(freq.astype(np.float32)[None], ((0, 0), (0, 80))))
    hbm, vmem = pl.BlockSpec(memory_space=pl.ANY), pl.BlockSpec(memory_space=pltpu.VMEM)
    n = N_CHUNK
    dma = pltpu.SemaphoreType.DMA
    out, dout = pl.pallas_call(
        kernel,
        out_shape=(jax.ShapeDtypeStruct((768, 1536), BF), jax.ShapeDtypeStruct((8, 1536), BF)),
        in_specs=[hbm, hbm, vmem, hbm, hbm, vmem, hbm, hbm, pl.BlockSpec(memory_space=pltpu.SMEM)],
        out_specs=(hbm, hbm),
        scratch_shapes=[
            pltpu.VMEM((12, 3072), BF), pltpu.VMEM((12, 1536), BF), pltpu.VMEM((12, 3072), BF), pltpu.VMEM((12, 1536), BF),
            pltpu.VMEM((8, 128), BF), pltpu.VMEM((8, 128), BF),
            pltpu.VMEM((6 * n, 4, 2, 4, 2, 24, 256), BF), pltpu.VMEM((4, 2, 4, 2, 8, 128), BF),
            pltpu.VMEM((784, 1536), BF), pltpu.VMEM((784, 1536), BF), pltpu.VMEM((784, 1536), F32),
            pltpu.VMEM((784, 384), F32), pltpu.VMEM((784, 384), F32),
            pltpu.VMEM((16, 784, 96), BF), pltpu.VMEM((8, 784, 96), BF), pltpu.VMEM((8, 784, 96), BF),
            pltpu.VMEM((784, 1536), BF), pltpu.VMEM((8, 512, 768), BF), pltpu.VMEM((8, 512, 768), BF),
            pltpu.VMEM((784, 1536), BF), pltpu.VMEM((5, 16, 8, 128), F32), pltpu.VMEM((4, 16, 8, 128), F32),
            dma((36 * n,)), dma((36 * n,)), dma((12 * n,)), dma((12 * n,)), dma((3,)), dma((3,)),
            dma((12,)), dma((12,)), dma((4,)), dma((4,)), dma((6,)), dma((7,)),
        ],
        compiler_params=pltpu.CompilerParams(
            collective_id=0, has_side_effects=True, vmem_limit_bytes=67043328),
        name="sublayer",
    )(wqkv, wo, norm_gain.reshape(1, 12), prefill_x, decode_x, freq, k_cache, v_cache, cache_len)
    return out, dout


def solution(mesh):
    rows = P(("dp", "shard"), None)
    in_specs = (rows, P("dp", None), P(("dp", "shard")), rows, rows,
                P("dp", "shard", None), P("dp", "shard", None), P("dp"))
    return jax.shard_map(per_device, mesh=mesh, in_specs=in_specs,
                         out_specs=(rows, P("dp", None)), check_vma=False)
```

```python
import jax
import jax.numpy as jnp
import numpy as np
from jax import lax
from jax.experimental import pallas as pl
from jax.experimental.pallas import tpu as pltpu
from jax.sharding import PartitionSpec as P

MESH = pl.DeviceIdType.MESH
H, KV, HD = 16, 8, 96
THETA, EPS, NEGATIVE = 100000.0, 1e-05, -1e30
SCALE = HD ** (-0.5)
ORDERS = (("x", "y", "z"), ("y", "z", "x"), ("z", "x", "y"))
N_CHUNK = 3
BF, F32 = jnp.bfloat16, jnp.float32


def coords():
    dp = lax.axis_index("dp"); sh = lax.axis_index("shard")
    core = sh % 2; yhi = (sh // 2) % 2; x = sh // 4
    ylo = dp % 2; z = dp // 2
    return {"x": x, "y": yhi * 2 + ylo, "z": z}, core

def device(c, core):
    return (c["z"] * 2 + c["y"] % 2, c["x"] * 4 + (c["y"] // 2) * 2 + core)

def moved(c, axis, by):
    d = dict(c); d[axis] = (c[axis] + by + 4) % 4
    return d

def block(ref, c, free):
    full = slice(None)
    z = full if "z" in free else c["z"]
    x = full if "x" in free else c["x"]
    ylo = full if "y" in free else c["y"] % 2
    yhi = full if "y" in free else c["y"] // 2
    return ref.at[z, ylo, x, yhi]

class Gather:
    def __init__(self, w, ssem, rsem, dsem_s, dsem_r):
        self.w, self.ssem, self.rsem, self.ds, self.dr = w, ssem, rsem, dsem_s, dsem_r
        self.c, self.core = coords()
        self.sent = []

    def part(self, t, k, core=None):
        core = self.core if core is None else core
        return self.w.at[t * 6 + core * 3 + k]

    def copy(self, t, k, f, s, right, origin):
        order = ORDERS[k]; axis = order[f]
        b = block(self.part(t, k), origin, order[:f])
        if s == 1:
            b = b.at[..., pl.ds(0 if right else 128, 128)]
        i = (((t * 3 + k) * 3 + f) * 2 + s) * 2 + (0 if right else 1)
        return pltpu.make_async_remote_copy(
            src_ref=b, dst_ref=b, send_sem=self.ssem.at[i], recv_sem=self.rsem.at[i],
            device_id=device(moved(self.c, axis, 1 if right else -1), self.core), device_id_type=MESH)

    def send(self, t, f, s):
        for k in range(3):
            axis = ORDERS[k][f]
            for right in (True, False):
                origin = self.c if s == 0 else moved(self.c, axis, -1 if right else 1)
                cp = self.copy(t, k, f, s, right, origin)
                cp.start(); self.sent.append(cp)

    def recv(self, t, f, s):
        for k in range(3):
            axis = ORDERS[k][f]
            for right in (True, False):
                by = (1 + s) * (-1 if right else 1)
                self.copy(t, k, f, s, right, moved(self.c, axis, by)).wait_recv()

    def d2d(self, t, k, j, core):
        order = ORDERS[k]
        b = block(self.part(t, k, core), moved(self.c, order[2], (0, -1, 1, 2)[j]), order[:2])
        i = (t * 3 + k) * 4 + j
        return pltpu.make_async_remote_copy(
            src_ref=b, dst_ref=b, send_sem=self.ds.at[i], recv_sem=self.dr.at[i],
            device_id=device(self.c, 1 - self.core), device_id_type=MESH)

    def give(self, t, js):
        for k in range(3):
            for j in js:
                cp = self.d2d(t, k, j, self.core); cp.start(); self.sent.append(cp)

    def take(self, t):
        for k in range(3):
            for j in range(4):
                self.d2d(t, k, j, 1 - self.core).wait_recv()

    def step(self, t, n):
        if n > 0:
            self.recv(t, (n - 1) // 2, (n - 1) % 2)
        if n < 6:
            self.send(t, n // 2, n % 2)
        if n == 4:
            self.give(t, (0,))
        if n == 5:
            self.give(t, (1, 2))
        if n == 6:
            self.give(t, (3,))

    def finish(self):
        for cp in self.sent:
            cp.wait_send()

def neighbours(c, core):
    out = [device(c, 1 - core)]
    for axis in ("x", "y", "z"):
        for by in (1, -1):
            out.append(device(moved(c, axis, by), core))
    return out + [partner(c, core, 1), partner(c, core, 3)]

def barrier(c, core):
    sem = pltpu.get_barrier_semaphore()
    for d in neighbours(c, core):
        pl.semaphore_signal(sem, inc=1, device_id=d, device_id_type=MESH)
    pl.semaphore_wait(sem, 9)

def both_rows(own, other, core):
    a, b = own[...].astype(F32), other[...].astype(F32)
    return jnp.concatenate([jnp.where(core == 0, a, b), jnp.where(core == 0, b, a)], axis=0)


def merge(t, own_q, other_q, own_o, other_o, w, c, core):
    if t == 2:
        cols = both_rows(own_o, other_o, core)
    else:
        a = both_rows(own_q, other_q, core)
        starts = [96 * (8 * t + 2 * g + e) + 48 * half for half in range(2) for e in range(2) for g in range(4)]
        starts += [1536 + 96 * (4 * t + h) + 48 * half for half in range(2) for h in range(4)]
        v = 2304 + 384 * t
        cols = jnp.concatenate([a[:, n : n + 48] for n in starts] + [a[:, v : v + 384]], axis=1)
    for k in range(3):
        part = jnp.where(core == 0, cols[:, 256 * k : 256 * k + 256], cols[:, 768 + 256 * k : 1024 + 256 * k])
        w[t * 6 + core * 3 + k, c["z"], c["y"] % 2, c["x"], c["y"] // 2] = part.astype(BF)


def gain_tile(gain, core):
    g = gain[...].astype(F32)
    zero = jnp.zeros((1, 116), F32)
    row = jnp.where(core == 0, jnp.concatenate([g, zero], axis=1),
                    jnp.concatenate([zero[:, :12], g, zero[:, :104]], axis=1))
    first = lax.broadcasted_iota(jnp.int32, (8, 128), 0) == 0
    return jnp.where(first, jnp.broadcast_to(row, (8, 128)), 0.0).astype(BF)


def angles(freq, clen, cos, sin):
    def put(start, size, at):
        a = at.astype(F32) * freq[...]
        rows = pl.ds(start, size)
        cos[rows, :] = jnp.concatenate([jnp.cos(a)[:, :48]] * 8, axis=1)
        sin[rows, :] = jnp.concatenate([jnp.sin(a)[:, :48]] * 8, axis=1)

    @pl.loop(0, 16)
    def _(i):
        put(pl.multiple_of(i * 48, 16), 48, lax.broadcasted_iota(jnp.int32, (48, 128), 0) + i * 48)

    row = lax.broadcasted_iota(jnp.int32, (16, 128), 0)
    at = jnp.zeros((16, 128), jnp.int32)
    for r in range(8):
        at = jnp.where(row == r, clen[r], at)
    put(768, 16, at)


class GainRing:
    def __init__(self, g, ssem, rsem):
        self.g, self.ssem, self.rsem = g, ssem, rsem
        self.c, self.core = coords()
        self.sent = []

    def copy(self, f, s, right, origin):
        order = ORDERS[0]
        b = block(self.g, origin, order[:f])
        i = (f * 2 + s) * 2 + (0 if right else 1)
        return pltpu.make_async_remote_copy(
            src_ref=b, dst_ref=b, send_sem=self.ssem.at[i], recv_sem=self.rsem.at[i],
            device_id=device(moved(self.c, order[f], 1 if right else -1), self.core), device_id_type=MESH)

    def step(self, n):
        axes = ORDERS[0]
        if n > 0:
            f, s = (n - 1) // 2, (n - 1) % 2
            for right in (True, False) if s == 0 else (True,):
                self.copy(f, s, right, moved(self.c, axes[f], (1 + s) * (-1 if right else 1))).wait_recv()
        if n < 6:
            f, s = n // 2, n % 2
            for right in (True, False) if s == 0 else (True,):
                cp = self.copy(f, s, right, self.c if s == 0 else moved(self.c, axes[f], -1))
                cp.start()
                self.sent.append(cp)

    def finish(self):
        for cp in self.sent:
            cp.wait_send()


def gain_row(g):
    tiles = g[...].astype(F32).reshape(64, 8, 128)
    values = jnp.sum(tiles, axis=1).astype(BF)
    column = lax.broadcasted_iota(jnp.int32, (64, 1536), 1)
    chip = lax.broadcasted_iota(jnp.int32, (64, 1536), 0) * 24
    mine = jnp.where((column >= chip) & (column < chip + 24), 1.0, 0.0).astype(BF)
    spread = lax.dot_general(values, mine, (((0,), (0,)), ((), ())), preferred_element_type=F32)
    n = lax.broadcasted_iota(jnp.int32, (128, 1536), 1).astype(F32)
    within = n - 24.0 * jnp.floor((n + 0.5) * (1.0 / 24.0))
    j = lax.broadcasted_iota(jnp.int32, (128, 1536), 0).astype(F32)
    return jnp.sum(jnp.where(within == j, spread, 0.0), axis=0, keepdims=True)


def normalize(xb, nb, gain):
    def scaled(start, size):
        wide = xb[pl.ds(start, size), :].astype(F32)
        factor = lax.rsqrt(jnp.mean(wide * wide, axis=-1, keepdims=True) + EPS)
        return wide * factor * gain

    @pl.loop(0, 12)
    def _(i):
        start = pl.multiple_of(i * 64, 64)
        nb[pl.ds(start, 64), :] = scaled(start, 64).astype(BF)

    nb[768:784, :] = jnp.concatenate([scaled(768, 8), jnp.zeros((8, 1536), F32)], axis=0).astype(BF)


def project(nb, w, u, t, lo, hi):
    @pl.loop(lo, hi)
    def _(j):
        rhs = w[t * 6 + j].reshape(1536, 256)
        u[:, pl.ds(pl.multiple_of(j * 256, 256), 256)] = jnp.dot(nb[...], rhs, preferred_element_type=F32)


def heads(u, cos, sin, qe, qo, kp, vp, t):
    def turned(lo, half, r, c, s):
        a, b = u[r, lo : lo + half], u[r, lo + half : lo + 2 * half]
        return (a * c - b * s).astype(BF), (b * c + a * s).astype(BF)

    def packed(a, b, lo):
        return jnp.concatenate([a[:, lo : lo + 96], b[:, lo : lo + 96], a[:, lo + 96 : lo + 192], b[:, lo + 96 : lo + 192]], axis=1)

    @pl.loop(0, 7)
    def _(i):
        r = pl.ds(pl.multiple_of(i * 112, 16), 112)
        c, s = cos[r, :], sin[r, :]
        a, b = turned(0, 384, r, c, s)
        qe[t, r, :] = packed(a, b, 0)
        qo[t, r, :] = packed(a, b, 192)
        a, b = turned(768, 192, r, c[:, :192], s[:, :192])
        kp[t, r, :] = packed(a, b, 0)
        vp[t, r, :] = u[r, 1152:1536].astype(BF)


def attend(qe, qo, kp, vp, attn, g):
    t, pair, j = g // 4, g % 4 // 2, g % 2
    win = slice(128 * pair, 128 * pair + 256)
    base = 64 * pair + 48 * j
    lane = lax.broadcasted_iota(jnp.int32, (16, 256), 1)
    mine = ((lane >= base) & (lane < base + 48)) | ((lane >= base + 96) & (lane < base + 144))
    mine = jnp.where(mine, 1.0, 0.0).astype(BF)[:1]
    off = 96 * (g % 4) - 128 * pair
    for i in range(3):
        lo, n = 256 * i, 256 * (i + 1)
        q = jnp.concatenate([qe[t, lo:n, win] * mine, qo[t, lo:n, win] * mine], axis=0)
        s = lax.dot_general(q, kp[t, 0:n, win], (((1,), (1,)), ((), ())), preferred_element_type=F32)
        row = lax.broadcasted_iota(jnp.int32, (512, 256), 0) & 255
        column = lax.broadcasted_iota(jnp.int32, (512, 256), 1)
        last = jnp.where(column <= row, s[:, lo:n], NEGATIVE)
        s = jnp.concatenate([s[:, :lo], last], axis=1) if i else last
        s = s * SCALE
        e = jnp.exp(s - jnp.max(s, axis=-1, keepdims=True))
        total = jnp.sum(e, axis=-1, keepdims=True)
        o = jnp.dot(e.astype(BF), vp[t, 0:n, win], preferred_element_type=F32)
        o = (o * (1.0 / total)).astype(BF)[:, off : off + 96]
        attn[lo:n, 192 * g : 192 * g + 192] = jnp.concatenate([o[:256], o[256:]], axis=1)


def decode_rows(ref, t, g):
    lo = 192 * (g // 2) + 48 * (g % 2)
    rows = jnp.concatenate([ref[t, 768:784, lo : lo + 48], ref[t, 768:784, lo + 96 : lo + 144]], axis=1)
    return rows.astype(F32)[:8]


def decode_queries(qe, qo):
    return jnp.stack([decode_rows((qe, qo)[h % 2], h // 8, h % 8 // 2) for h in range(16)])


def decode_block(qe, qo, kc, vc, clen, pk):
    q = decode_queries(qe, qo)
    lane = lax.broadcasted_iota(jnp.int32, (16, 768), 1)
    first = (lax.broadcasted_iota(jnp.int32, (16, 768), 0) // 2) * 96
    mine = (lane >= first) & (lane < first + 96)
    at = lax.axis_index("shard") * 512 + lax.broadcasted_iota(jnp.int32, (16, 512), 1)
    for r in range(8):
        one = q[:, r, :]
        spread = jnp.concatenate([one] * 8, axis=1)
        qw = jnp.where(mine, spread, 0.0).astype(BF)
        s = lax.dot_general(qw, kc[r], (((1,), (1,)), ((), ())), preferred_element_type=F32) * SCALE
        live = at < clen[r]
        s = jnp.where(live, s, NEGATIVE)
        peak = jnp.max(s, axis=-1, keepdims=True)
        e = jnp.where(live, jnp.exp(s - peak), 0.0)
        total = jnp.sum(e, axis=-1, keepdims=True)
        every = jnp.where(mine, jnp.dot(e.astype(BF), vc[r], preferred_element_type=F32), 0.0)
        acc = every[:, 0:96]
        for g in range(1, 8):
            acc = acc + every[:, 96 * g : 96 * g + 96]
        pk[:, r, :] = jnp.concatenate(
            [acc, jnp.broadcast_to(peak, (16, 16)), jnp.broadcast_to(total, (16, 16))], axis=1)


class Combine:
    def __init__(self, pk, rv, ssem, rsem):
        self.pk, self.rv, self.ssem, self.rsem = pk, rv, ssem, rsem
        self.sent = []

    def copy(self, j):
        c, core = coords()
        return pltpu.make_async_remote_copy(
            src_ref=self.pk.at[j], dst_ref=self.rv.at[j], send_sem=self.ssem.at[j], recv_sem=self.rsem.at[j],
            device_id=partner(c, core, j), device_id_type=MESH)

    def send(self, j):
        cp = self.copy(j)
        cp.start()
        self.sent.append(cp)

    def add(self, j):
        self.copy(j).wait_recv()
        a, b = self.pk[j], self.rv[j]
        pa, pb = a[:, :, 96:97], b[:, :, 96:97]
        top = jnp.maximum(pa, pb)
        both = a * jnp.exp(pa - top) + b * jnp.exp(pb - top)
        lane = lax.broadcasted_iota(jnp.int32, both.shape, 2)
        self.pk[j + 1] = jnp.where((lane >= 96) & (lane < 112), top, both)

    def finish(self):
        for cp in self.sent:
            cp.wait_send()


def partner(c, core, j):
    if j == 0:
        return device(c, 1 - core)
    if j == 1:
        return device(moved(c, "y", 2), core)
    if j == 2:
        return device({**c, "x": c["x"] + 1 - 2 * (c["x"] % 2)}, core)
    return device(moved(c, "x", 2), core)


def decode_mix(pk, qe, qo, kp, vp, attn):
    a = pk[4]
    acc, peak, total = a[:, :, 0:96], a[:, :, 96:97], a[:, :, 112:113]
    q = decode_queries(qe, qo)
    keys = jnp.stack([decode_rows(kp, h // 8, h % 8 // 2) for h in range(16)])
    values = jnp.stack([vp[h // 8, 768:784, 96 * (h % 8 // 2) : 96 * (h % 8 // 2) + 96].astype(F32)[:8] for h in range(16)])
    own = jnp.sum(q * keys, axis=-1, keepdims=True) * SCALE
    top = jnp.maximum(peak, own)
    old, new = jnp.exp(peak - top), jnp.exp(own - top)
    mix = (acc * old + new * values) / (total * old + new)
    zero = jnp.zeros((8, 96), F32)
    for h in range(16):
        attn[768:784, 96 * h : 96 * h + 96] = jnp.concatenate([mix[h], zero], axis=0).astype(BF)


def kernel(wq_ref, wo_ref, gain_ref, x_ref, dx_ref, freq, k_ref, v_ref, clen, out_ref, dout_ref,
           own_q, own_o, other_q, other_o, gown, gother, w, g, xb, nb, u, cos, sin, qe, qo, kp, vp, attn, kc, vc, o, pk, rv,
           ssem, rsem, ds, dr, ps, pr, gs, gr, cs, cr, lsem, osem):
    c, core = coords()
    loads = [pltpu.make_async_copy(s, d, lsem.at[i]) for i, (s, d) in enumerate((
        (wq_ref, own_q), (wo_ref, own_o), (x_ref, xb.at[pl.ds(0, 768)]), (dx_ref, xb.at[pl.ds(768, 8)]),
        (k_ref, kc), (v_ref, vc)))]
    for cp in loads[:2]:
        cp.start()
    gown[...] = gain_tile(gain_ref, core)
    barrier(c, core)
    pre = [pltpu.make_async_remote_copy(
        src_ref=s, dst_ref=d, send_sem=ps.at[i], recv_sem=pr.at[i],
        device_id=device(c, 1 - core), device_id_type=MESH)
        for i, (s, d) in enumerate(((wq_ref, other_q), (wo_ref, other_o), (gown, gother)))]
    for cp in pre:
        cp.start()
    for cp in loads[2:]:
        cp.start()
    for cp in loads[:2]:
        cp.wait()
    for cp in pre:
        cp.wait()
    g[c["z"], c["y"] % 2, c["x"], c["y"] // 2] = (gown[...].astype(F32) + gother[...].astype(F32)).astype(BF)
    G = Gather(w, ssem, rsem, ds, dr)
    R = GainRing(g, gs, gr)
    D = Combine(pk, rv, cs, cr)

    def ticks(tick):
        R.step(tick)
        for t in range(N_CHUNK):
            if tick == t:
                merge(t, own_q, other_q, own_o, other_o, w, c, core)
            if tick >= t:
                G.step(t, tick - t)

    for tick in range(5):
        ticks(tick)
    angles(freq, clen, cos, sin)
    ticks(5)
    for cp in loads[2:4]:
        cp.wait()
    R.step(6)
    normalize(xb, nb, gain_row(g))
    G.step(0, 6)
    G.take(0)
    project(nb, w, u, 0, 0, 3)
    G.step(1, 5)
    G.step(2, 4)
    project(nb, w, u, 0, 3, 6)
    G.step(1, 6)
    heads(u, cos, sin, qe, qo, kp, vp, 0)
    G.step(2, 5)
    attend(qe, qo, kp, vp, attn, 0)
    G.take(1)
    project(nb, w, u, 1, 0, 3)
    G.step(2, 6)
    project(nb, w, u, 1, 3, 6)
    heads(u, cos, sin, qe, qo, kp, vp, 1)
    for cp in loads[4:]:
        cp.wait()
    decode_block(qe, qo, kc, vc, clen, pk.at[0])
    for j, groups in enumerate(((1, 2), (3, 4), (5, 6), (7,))):
        D.send(j)
        for g_ in groups:
            attend(qe, qo, kp, vp, attn, g_)
        D.add(j)
    decode_mix(pk, qe, qo, kp, vp, attn)
    G.take(2)

    def leaving(j):
        cols = pl.ds(pl.multiple_of(j * 256, 256), 256)
        return pltpu.make_async_copy(o.at[pl.ds(0, 768), cols], out_ref.at[:, cols], osem.at[j])

    @pl.loop(0, 6)
    def _(j):
        rhs = w[12 + j].reshape(1536, 256)
        o[:, pl.ds(pl.multiple_of(j * 256, 256), 256)] = jnp.dot(
            attn[...], rhs, preferred_element_type=F32).astype(BF)
        leaving(j).start()

    outs = [leaving(j) for j in range(6)]
    outs.append(pltpu.make_async_copy(o.at[pl.ds(768, 8)], dout_ref, osem.at[6]))
    outs[6].start()
    G.finish()
    R.finish()
    D.finish()
    for cp in outs:
        cp.wait()


def per_device(prefill_x, decode_x, norm_gain, wqkv, wo, k_cache, v_cache, cache_len):
    freq = np.power(np.float32(THETA), -np.arange(48, dtype=np.float32) * np.float32(2.0 / HD))
    freq = jnp.asarray(np.pad(freq.astype(np.float32)[None], ((0, 0), (0, 80))))
    hbm, vmem = pl.BlockSpec(memory_space=pl.ANY), pl.BlockSpec(memory_space=pltpu.VMEM)
    n = N_CHUNK
    dma = pltpu.SemaphoreType.DMA
    out, dout = pl.pallas_call(
        kernel,
        out_shape=(jax.ShapeDtypeStruct((768, 1536), BF), jax.ShapeDtypeStruct((8, 1536), BF)),
        in_specs=[hbm, hbm, vmem, hbm, hbm, vmem, hbm, hbm, pl.BlockSpec(memory_space=pltpu.SMEM)],
        out_specs=(hbm, hbm),
        scratch_shapes=[
            pltpu.VMEM((12, 3072), BF), pltpu.VMEM((12, 1536), BF), pltpu.VMEM((12, 3072), BF), pltpu.VMEM((12, 1536), BF),
            pltpu.VMEM((8, 128), BF), pltpu.VMEM((8, 128), BF),
            pltpu.VMEM((6 * n, 4, 2, 4, 2, 24, 256), BF), pltpu.VMEM((4, 2, 4, 2, 8, 128), BF),
            pltpu.VMEM((784, 1536), BF), pltpu.VMEM((784, 1536), BF), pltpu.VMEM((784, 1536), F32),
            pltpu.VMEM((784, 384), F32), pltpu.VMEM((784, 384), F32),
            pltpu.VMEM((2, 784, 384), BF), pltpu.VMEM((2, 784, 384), BF),
            pltpu.VMEM((2, 784, 384), BF), pltpu.VMEM((2, 784, 384), BF),
            pltpu.VMEM((784, 1536), BF), pltpu.VMEM((8, 512, 768), BF), pltpu.VMEM((8, 512, 768), BF),
            pltpu.VMEM((784, 1536), BF), pltpu.VMEM((5, 16, 8, 128), F32), pltpu.VMEM((4, 16, 8, 128), F32),
            dma((36 * n,)), dma((36 * n,)), dma((12 * n,)), dma((12 * n,)), dma((3,)), dma((3,)),
            dma((12,)), dma((12,)), dma((4,)), dma((4,)), dma((6,)), dma((7,)),
        ],
        compiler_params=pltpu.CompilerParams(
            collective_id=0, has_side_effects=True, vmem_limit_bytes=67043328),
        name="sublayer",
    )(wqkv, wo, norm_gain.reshape(1, 12), prefill_x, decode_x, freq, k_cache, v_cache, cache_len)
    return out, dout


def solution(mesh):
    rows = P(("dp", "shard"), None)
    in_specs = (rows, P("dp", None), P(("dp", "shard")), rows, rows,
                P("dp", "shard", None), P("dp", "shard", None), P("dp"))
    return jax.shard_map(per_device, mesh=mesh, in_specs=in_specs,
                         out_specs=(rows, P("dp", None)), check_vma=False)
```

```python
import jax
import jax.numpy as jnp
import numpy as np
from jax import lax
from jax.experimental import pallas as pl
from jax.experimental.pallas import tpu as pltpu
from jax.sharding import PartitionSpec as P

MESH = pl.DeviceIdType.MESH
H, KV, HD = 16, 8, 96
THETA, EPS, NEGATIVE = 100000.0, 1e-05, -1e30
SCALE = HD ** (-0.5)
RATE = SCALE * 1.4426950408889634
ORDERS = (("x", "y", "z"), ("y", "z", "x"), ("z", "x", "y"))
N_CHUNK = 3
BF, F32 = jnp.bfloat16, jnp.float32


def coords():
    dp = lax.axis_index("dp"); sh = lax.axis_index("shard")
    core = sh % 2; yhi = (sh // 2) % 2; x = sh // 4
    ylo = dp % 2; z = dp // 2
    return {"x": x, "y": yhi * 2 + ylo, "z": z}, core

def device(c, core):
    return (c["z"] * 2 + c["y"] % 2, c["x"] * 4 + (c["y"] // 2) * 2 + core)

def moved(c, axis, by):
    d = dict(c); d[axis] = (c[axis] + by + 4) % 4
    return d

def block(ref, c, free):
    full = slice(None)
    z = full if "z" in free else c["z"]
    x = full if "x" in free else c["x"]
    ylo = full if "y" in free else c["y"] % 2
    yhi = full if "y" in free else c["y"] // 2
    return ref.at[z, ylo, x, yhi]

class Gather:
    def __init__(self, w, ssem, rsem, dsem_s, dsem_r):
        self.w, self.ssem, self.rsem, self.ds, self.dr = w, ssem, rsem, dsem_s, dsem_r
        self.c, self.core = coords()
        self.sent = []

    def part(self, t, k, core=None):
        core = self.core if core is None else core
        return self.w.at[t * 6 + core * 3 + k]

    def copy(self, t, k, f, s, right, origin):
        order = ORDERS[k]; axis = order[f]
        b = block(self.part(t, k), origin, order[:f])
        if s == 1:
            b = b.at[..., pl.ds(0 if right else 128, 128)]
        i = (((t * 3 + k) * 3 + f) * 2 + s) * 2 + (0 if right else 1)
        return pltpu.make_async_remote_copy(
            src_ref=b, dst_ref=b, send_sem=self.ssem.at[i], recv_sem=self.rsem.at[i],
            device_id=device(moved(self.c, axis, 1 if right else -1), self.core), device_id_type=MESH)

    def send(self, t, f, s):
        for k in range(3):
            axis = ORDERS[k][f]
            for right in (True, False):
                origin = self.c if s == 0 else moved(self.c, axis, -1 if right else 1)
                cp = self.copy(t, k, f, s, right, origin)
                cp.start(); self.sent.append(cp)

    def recv(self, t, f, s):
        for k in range(3):
            axis = ORDERS[k][f]
            for right in (True, False):
                by = (1 + s) * (-1 if right else 1)
                self.copy(t, k, f, s, right, moved(self.c, axis, by)).wait_recv()

    def d2d(self, t, k, j, core):
        order = ORDERS[k]
        b = block(self.part(t, k, core), moved(self.c, order[2], (0, -1, 1, 2)[j]), order[:2])
        i = (t * 3 + k) * 4 + j
        return pltpu.make_async_remote_copy(
            src_ref=b, dst_ref=b, send_sem=self.ds.at[i], recv_sem=self.dr.at[i],
            device_id=device(self.c, 1 - self.core), device_id_type=MESH)

    def give(self, t, js):
        for k in range(3):
            for j in js:
                cp = self.d2d(t, k, j, self.core); cp.start(); self.sent.append(cp)

    def take(self, t):
        for k in range(3):
            for j in range(4):
                self.d2d(t, k, j, 1 - self.core).wait_recv()

    def step(self, t, n):
        if n > 0:
            self.recv(t, (n - 1) // 2, (n - 1) % 2)
        if n < 6:
            self.send(t, n // 2, n % 2)
        if n == 4:
            self.give(t, (0,))
        if n == 5:
            self.give(t, (1, 2))
        if n == 6:
            self.give(t, (3,))

    def finish(self):
        for cp in self.sent:
            cp.wait_send()

def neighbours(c, core):
    out = [device(c, 1 - core)]
    for axis in ("x", "y", "z"):
        for by in (1, -1):
            out.append(device(moved(c, axis, by), core))
    return out + [partner(c, core, 1), partner(c, core, 3)]

def barrier(c, core):
    sem = pltpu.get_barrier_semaphore()
    for d in neighbours(c, core):
        pl.semaphore_signal(sem, inc=1, device_id=d, device_id_type=MESH)
    pl.semaphore_wait(sem, 9)

def both_rows(own, other, core):
    a, b = own[...].astype(F32), other[...].astype(F32)
    return jnp.concatenate([jnp.where(core == 0, a, b), jnp.where(core == 0, b, a)], axis=0)


def merge(t, own_q, other_q, own_o, other_o, w, c, core):
    if t == 2:
        cols = both_rows(own_o, other_o, core)
    else:
        a = both_rows(own_q, other_q, core)
        starts = [96 * (8 * t + 2 * g + e) + 48 * half for half in range(2) for e in range(2) for g in range(4)]
        starts += [1536 + 96 * (4 * t + h) + 48 * half for half in range(2) for h in range(4)]
        v = 2304 + 384 * t
        cols = jnp.concatenate([a[:, n : n + 48] for n in starts] + [a[:, v : v + 384]], axis=1)
    for k in range(3):
        part = jnp.where(core == 0, cols[:, 256 * k : 256 * k + 256], cols[:, 768 + 256 * k : 1024 + 256 * k])
        w[t * 6 + core * 3 + k, c["z"], c["y"] % 2, c["x"], c["y"] // 2] = part.astype(BF)


def gain_tile(gain, core):
    g = gain[...].astype(F32)
    zero = jnp.zeros((1, 116), F32)
    row = jnp.where(core == 0, jnp.concatenate([g, zero], axis=1),
                    jnp.concatenate([zero[:, :12], g, zero[:, :104]], axis=1))
    first = lax.broadcasted_iota(jnp.int32, (8, 128), 0) == 0
    return jnp.where(first, jnp.broadcast_to(row, (8, 128)), 0.0).astype(BF)


def angles(freq, clen, cos, sin):
    def put(start, size, at):
        a = at.astype(F32) * freq[...]
        rows = pl.ds(start, size)
        cos[rows, :] = jnp.concatenate([jnp.cos(a)[:, :48]] * 8, axis=1)
        sin[rows, :] = jnp.concatenate([jnp.sin(a)[:, :48]] * 8, axis=1)

    @pl.loop(0, 16)
    def _(i):
        put(pl.multiple_of(i * 48, 16), 48, lax.broadcasted_iota(jnp.int32, (48, 128), 0) + i * 48)

    row = lax.broadcasted_iota(jnp.int32, (16, 128), 0)
    at = jnp.zeros((16, 128), jnp.int32)
    for r in range(8):
        at = jnp.where(row == r, clen[r], at)
    put(768, 16, at)


class GainRing:
    def __init__(self, g, ssem, rsem):
        self.g, self.ssem, self.rsem = g, ssem, rsem
        self.c, self.core = coords()
        self.sent = []

    def copy(self, f, s, right, origin):
        order = ORDERS[0]
        b = block(self.g, origin, order[:f])
        i = (f * 2 + s) * 2 + (0 if right else 1)
        return pltpu.make_async_remote_copy(
            src_ref=b, dst_ref=b, send_sem=self.ssem.at[i], recv_sem=self.rsem.at[i],
            device_id=device(moved(self.c, order[f], 1 if right else -1), self.core), device_id_type=MESH)

    def step(self, n):
        axes = ORDERS[0]
        if n > 0:
            f, s = (n - 1) // 2, (n - 1) % 2
            for right in (True, False) if s == 0 else (True,):
                self.copy(f, s, right, moved(self.c, axes[f], (1 + s) * (-1 if right else 1))).wait_recv()
        if n < 6:
            f, s = n // 2, n % 2
            for right in (True, False) if s == 0 else (True,):
                cp = self.copy(f, s, right, self.c if s == 0 else moved(self.c, axes[f], -1))
                cp.start()
                self.sent.append(cp)

    def finish(self):
        for cp in self.sent:
            cp.wait_send()


def gain_row(g):
    tiles = g[...].astype(F32).reshape(64, 8, 128)
    values = jnp.sum(tiles, axis=1).astype(BF)
    column = lax.broadcasted_iota(jnp.int32, (64, 1536), 1)
    chip = lax.broadcasted_iota(jnp.int32, (64, 1536), 0) * 24
    mine = jnp.where((column >= chip) & (column < chip + 24), 1.0, 0.0).astype(BF)
    spread = lax.dot_general(values, mine, (((0,), (0,)), ((), ())), preferred_element_type=F32)
    n = lax.broadcasted_iota(jnp.int32, (128, 1536), 1).astype(F32)
    within = n - 24.0 * jnp.floor((n + 0.5) * (1.0 / 24.0))
    j = lax.broadcasted_iota(jnp.int32, (128, 1536), 0).astype(F32)
    return jnp.sum(jnp.where(within == j, spread, 0.0), axis=0, keepdims=True)


def normalize(xb, nb, gain):
    def scaled(start, size):
        wide = xb[pl.ds(start, size), :].astype(F32)
        factor = lax.rsqrt(jnp.mean(wide * wide, axis=-1, keepdims=True) + EPS)
        return wide * factor * gain

    @pl.loop(0, 12)
    def _(i):
        start = pl.multiple_of(i * 64, 64)
        nb[pl.ds(start, 64), :] = scaled(start, 64).astype(BF)

    nb[768:784, :] = jnp.concatenate([scaled(768, 8), jnp.zeros((8, 1536), F32)], axis=0).astype(BF)


def project(nb, w, u, t, core):
    @pl.loop(0, 3)
    def _(i):
        j = core * 3 + i
        rhs = w[t * 6 + j].reshape(1536, 256)
        u[:, pl.ds(pl.multiple_of(j * 256, 256), 256)] = jnp.dot(nb[...], rhs, preferred_element_type=F32)


def heads(u, cos, sin, qe, qo, kp, vp, t):
    def turned(lo, half, r, c, s):
        a, b = u[r, lo : lo + half], u[r, lo + half : lo + 2 * half]
        return (a * c - b * s).astype(BF), (b * c + a * s).astype(BF)

    def packed(a, b, lo):
        return jnp.concatenate([a[:, lo : lo + 96], b[:, lo : lo + 96], a[:, lo + 96 : lo + 192], b[:, lo + 96 : lo + 192]], axis=1)

    @pl.loop(0, 7)
    def _(i):
        r = pl.ds(pl.multiple_of(i * 112, 16), 112)
        c, s = cos[r, :], sin[r, :]
        a, b = turned(0, 384, r, c, s)
        qe[t, r, :] = packed(a, b, 0)
        qo[t, r, :] = packed(a, b, 192)
        a, b = turned(768, 192, r, c[:, :192], s[:, :192])
        kp[t, r, :] = packed(a, b, 0)
        vp[t, r, :] = u[r, 1152:1536].astype(BF)


def attend(qe, qo, kp, vp, attn, g):
    t, pair, j = g // 4, g % 4 // 2, g % 2
    win = slice(128 * pair, 128 * pair + 256)
    base = 64 * pair + 48 * j
    lane = lax.broadcasted_iota(jnp.int32, (16, 256), 1)
    mine = ((lane >= base) & (lane < base + 48)) | ((lane >= base + 96) & (lane < base + 144))
    mine = jnp.where(mine, 1.0, 0.0).astype(BF)[:1]
    off = 96 * (g % 4) - 128 * pair
    for i in range(3):
        lo, n = 256 * i, 256 * (i + 1)
        q = jnp.concatenate([qe[t, lo:n, win] * mine, qo[t, lo:n, win] * mine], axis=0)
        s = lax.dot_general(q, kp[t, 0:n, win], (((1,), (1,)), ((), ())), preferred_element_type=F32)
        row = lax.broadcasted_iota(jnp.int32, (512, 256), 0) & 255
        column = lax.broadcasted_iota(jnp.int32, (512, 256), 1)
        last = jnp.where(column <= row, s[:, lo:n], NEGATIVE)
        s = jnp.concatenate([s[:, :lo], last], axis=1) if i else last
        e = jnp.exp2(s * RATE - jnp.max(s, axis=-1, keepdims=True) * RATE)
        total = jnp.sum(e, axis=-1, keepdims=True)
        o = jnp.dot(e.astype(BF), vp[t, 0:n, win], preferred_element_type=F32)
        o = (o * (1.0 / total)).astype(BF)[:, off : off + 96]
        attn[lo:n, 192 * g : 192 * g + 192] = jnp.concatenate([o[:256], o[256:]], axis=1)


def decode_rows(ref, t, g):
    lo = 192 * (g // 2) + 48 * (g % 2)
    rows = jnp.concatenate([ref[t, 768:784, lo : lo + 48], ref[t, 768:784, lo + 96 : lo + 144]], axis=1)
    return rows.astype(F32)[:8]


def decode_queries(qe, qo):
    return jnp.stack([decode_rows((qe, qo)[h % 2], h // 8, h % 8 // 2) for h in range(16)])


def decode_block(qe, qo, kc, vc, clen, pk):
    q = decode_queries(qe, qo)
    lane = lax.broadcasted_iota(jnp.int32, (16, 768), 1)
    first = (lax.broadcasted_iota(jnp.int32, (16, 768), 0) // 2) * 96
    mine = (lane >= first) & (lane < first + 96)
    at = lax.axis_index("shard") * 512 + lax.broadcasted_iota(jnp.int32, (16, 512), 1)
    for r in range(8):
        one = q[:, r, :]
        spread = jnp.concatenate([one] * 8, axis=1)
        qw = jnp.where(mine, spread, 0.0).astype(BF)
        s = lax.dot_general(qw, kc[r], (((1,), (1,)), ((), ())), preferred_element_type=F32) * SCALE
        live = at < clen[r]
        s = jnp.where(live, s, NEGATIVE)
        peak = jnp.max(s, axis=-1, keepdims=True)
        e = jnp.where(live, jnp.exp(s - peak), 0.0)
        total = jnp.sum(e, axis=-1, keepdims=True)
        every = jnp.where(mine, jnp.dot(e.astype(BF), vc[r], preferred_element_type=F32), 0.0)
        acc = every[:, 0:96]
        for g in range(1, 8):
            acc = acc + every[:, 96 * g : 96 * g + 96]
        pk[:, r, :] = jnp.concatenate(
            [acc, jnp.broadcast_to(peak, (16, 16)), jnp.broadcast_to(total, (16, 16))], axis=1)


class Combine:
    def __init__(self, pk, rv, ssem, rsem):
        self.pk, self.rv, self.ssem, self.rsem = pk, rv, ssem, rsem
        self.sent = []

    def copy(self, j):
        c, core = coords()
        return pltpu.make_async_remote_copy(
            src_ref=self.pk.at[j], dst_ref=self.rv.at[j], send_sem=self.ssem.at[j], recv_sem=self.rsem.at[j],
            device_id=partner(c, core, j), device_id_type=MESH)

    def send(self, j):
        cp = self.copy(j)
        cp.start()
        self.sent.append(cp)

    def add(self, j):
        self.copy(j).wait_recv()
        a, b = self.pk[j], self.rv[j]
        pa, pb = a[:, :, 96:97], b[:, :, 96:97]
        top = jnp.maximum(pa, pb)
        both = a * jnp.exp(pa - top) + b * jnp.exp(pb - top)
        lane = lax.broadcasted_iota(jnp.int32, both.shape, 2)
        self.pk[j + 1] = jnp.where((lane >= 96) & (lane < 112), top, both)

    def finish(self):
        for cp in self.sent:
            cp.wait_send()


def partner(c, core, j):
    if j == 0:
        return device(c, 1 - core)
    if j == 1:
        return device(moved(c, "y", 2), core)
    if j == 2:
        return device({**c, "x": c["x"] + 1 - 2 * (c["x"] % 2)}, core)
    return device(moved(c, "x", 2), core)


def decode_mix(pk, qe, qo, kp, vp, attn):
    a = pk[4]
    acc, peak, total = a[:, :, 0:96], a[:, :, 96:97], a[:, :, 112:113]
    q = decode_queries(qe, qo)
    keys = jnp.stack([decode_rows(kp, h // 8, h % 8 // 2) for h in range(16)])
    values = jnp.stack([vp[h // 8, 768:784, 96 * (h % 8 // 2) : 96 * (h % 8 // 2) + 96].astype(F32)[:8] for h in range(16)])
    own = jnp.sum(q * keys, axis=-1, keepdims=True) * SCALE
    top = jnp.maximum(peak, own)
    old, new = jnp.exp(peak - top), jnp.exp(own - top)
    mix = (acc * old + new * values) / (total * old + new)
    zero = jnp.zeros((8, 96), F32)
    for h in range(16):
        attn[768:784, 96 * h : 96 * h + 96] = jnp.concatenate([mix[h], zero], axis=0).astype(BF)


def kernel(wq_ref, wo_ref, gain_ref, x_ref, dx_ref, freq, k_ref, v_ref, clen, out_ref, dout_ref,
           own_q, own_o, other_q, other_o, gown, gother, w, g, xb, nb, u, cos, sin, qe, qo, kp, vp, attn, kc, vc, o, pk, rv,
           ssem, rsem, ds, dr, ps, pr, gs, gr, cs, cr, lsem, osem):
    c, core = coords()
    loads = [pltpu.make_async_copy(s, d, lsem.at[i]) for i, (s, d) in enumerate((
        (wq_ref, own_q), (wo_ref, own_o), (x_ref, xb.at[pl.ds(0, 768)]), (dx_ref, xb.at[pl.ds(768, 8)]),
        (k_ref, kc), (v_ref, vc)))]
    for cp in loads[:2]:
        cp.start()
    gown[...] = gain_tile(gain_ref, core)
    barrier(c, core)
    pre = [pltpu.make_async_remote_copy(
        src_ref=s, dst_ref=d, send_sem=ps.at[i], recv_sem=pr.at[i],
        device_id=device(c, 1 - core), device_id_type=MESH)
        for i, (s, d) in enumerate(((wq_ref, other_q), (wo_ref, other_o), (gown, gother)))]
    for cp in pre:
        cp.start()
    for cp in loads[:2]:
        cp.wait()
    for cp in pre:
        cp.wait()
    g[c["z"], c["y"] % 2, c["x"], c["y"] // 2] = (gown[...].astype(F32) + gother[...].astype(F32)).astype(BF)
    G = Gather(w, ssem, rsem, ds, dr)
    R = GainRing(g, gs, gr)
    D = Combine(pk, rv, cs, cr)

    def ticks(tick):
        R.step(tick)
        for t in range(N_CHUNK):
            if tick == t:
                merge(t, own_q, other_q, own_o, other_o, w, c, core)
            if tick >= t:
                G.step(t, tick - t)

    for tick in range(5):
        ticks(tick)
        if tick == 2:
            for cp in loads[2:]:
                cp.start()
    angles(freq, clen, cos, sin)
    ticks(5)
    for cp in loads[2:4]:
        cp.wait()
    R.step(6)
    normalize(xb, nb, gain_row(g))
    G.step(0, 6)
    project(nb, w, u, 0, core)
    G.step(1, 5)
    G.step(2, 4)
    G.take(0)
    project(nb, w, u, 0, 1 - core)
    G.step(1, 6)
    heads(u, cos, sin, qe, qo, kp, vp, 0)
    G.step(2, 5)
    attend(qe, qo, kp, vp, attn, 0)
    project(nb, w, u, 1, core)
    G.step(2, 6)
    G.take(1)
    project(nb, w, u, 1, 1 - core)
    heads(u, cos, sin, qe, qo, kp, vp, 1)
    for cp in loads[4:]:
        cp.wait()
    decode_block(qe, qo, kc, vc, clen, pk.at[0])
    for j, groups in enumerate(((1, 2), (3, 4), (5, 6), (7,))):
        D.send(j)
        for g_ in groups:
            attend(qe, qo, kp, vp, attn, g_)
        D.add(j)
    decode_mix(pk, qe, qo, kp, vp, attn)
    G.take(2)

    def leaving(j):
        cols = pl.ds(pl.multiple_of(j * 256, 256), 256)
        return pltpu.make_async_copy(o.at[pl.ds(0, 768), cols], out_ref.at[:, cols], osem.at[j])

    @pl.loop(0, 6)
    def _(j):
        rhs = w[12 + j].reshape(1536, 256)
        o[:, pl.ds(pl.multiple_of(j * 256, 256), 256)] = jnp.dot(
            attn[...], rhs, preferred_element_type=F32).astype(BF)
        leaving(j).start()

    outs = [leaving(j) for j in range(6)]
    outs.append(pltpu.make_async_copy(o.at[pl.ds(768, 8)], dout_ref, osem.at[6]))
    outs[6].start()
    G.finish()
    R.finish()
    D.finish()
    for cp in outs:
        cp.wait()


def per_device(prefill_x, decode_x, norm_gain, wqkv, wo, k_cache, v_cache, cache_len):
    freq = np.power(np.float32(THETA), -np.arange(48, dtype=np.float32) * np.float32(2.0 / HD))
    freq = jnp.asarray(np.pad(freq.astype(np.float32)[None], ((0, 0), (0, 80))))
    hbm, vmem = pl.BlockSpec(memory_space=pl.ANY), pl.BlockSpec(memory_space=pltpu.VMEM)
    n = N_CHUNK
    dma = pltpu.SemaphoreType.DMA
    out, dout = pl.pallas_call(
        kernel,
        out_shape=(jax.ShapeDtypeStruct((768, 1536), BF), jax.ShapeDtypeStruct((8, 1536), BF)),
        in_specs=[hbm, hbm, vmem, hbm, hbm, vmem, hbm, hbm, pl.BlockSpec(memory_space=pltpu.SMEM)],
        out_specs=(hbm, hbm),
        scratch_shapes=[
            pltpu.VMEM((12, 3072), BF), pltpu.VMEM((12, 1536), BF), pltpu.VMEM((12, 3072), BF), pltpu.VMEM((12, 1536), BF),
            pltpu.VMEM((8, 128), BF), pltpu.VMEM((8, 128), BF),
            pltpu.VMEM((6 * n, 4, 2, 4, 2, 24, 256), BF), pltpu.VMEM((4, 2, 4, 2, 8, 128), BF),
            pltpu.VMEM((784, 1536), BF), pltpu.VMEM((784, 1536), BF), pltpu.VMEM((784, 1536), F32),
            pltpu.VMEM((784, 384), F32), pltpu.VMEM((784, 384), F32),
            pltpu.VMEM((2, 784, 384), BF), pltpu.VMEM((2, 784, 384), BF),
            pltpu.VMEM((2, 784, 384), BF), pltpu.VMEM((2, 784, 384), BF),
            pltpu.VMEM((784, 1536), BF), pltpu.VMEM((8, 512, 768), BF), pltpu.VMEM((8, 512, 768), BF),
            pltpu.VMEM((784, 1536), BF), pltpu.VMEM((5, 16, 8, 128), F32), pltpu.VMEM((4, 16, 8, 128), F32),
            dma((36 * n,)), dma((36 * n,)), dma((12 * n,)), dma((12 * n,)), dma((3,)), dma((3,)),
            dma((12,)), dma((12,)), dma((4,)), dma((4,)), dma((6,)), dma((7,)),
        ],
        compiler_params=pltpu.CompilerParams(
            collective_id=0, has_side_effects=True, vmem_limit_bytes=67043328),
        name="sublayer",
    )(wqkv, wo, norm_gain.reshape(1, 12), prefill_x, decode_x, freq, k_cache, v_cache, cache_len)
    return out, dout


def solution(mesh):
    rows = P(("dp", "shard"), None)
    in_specs = (rows, P("dp", None), P(("dp", "shard")), rows, rows,
                P("dp", "shard", None), P("dp", "shard", None), P("dp"))
    return jax.shard_map(per_device, mesh=mesh, in_specs=in_specs,
                         out_specs=(rows, P("dp", None)), check_vma=False)
```

```python
import jax
import jax.numpy as jnp
import numpy as np
from jax import lax
from jax.experimental import pallas as pl
from jax.experimental.pallas import tpu as pltpu
from jax.sharding import PartitionSpec as P

MESH = pl.DeviceIdType.MESH
H, KV, HD = 16, 8, 96
THETA, EPS, NEGATIVE = 100000.0, 1e-05, -1e30
SCALE = HD ** (-0.5)
RATE = SCALE * 1.4426950408889634
ORDERS = (("x", "y", "z"), ("y", "z", "x"), ("z", "x", "y"))
N_CHUNK = 3
PLAN = ((0, 0), (1, 0), (1, 1), (2, 0), (2, 1))
BF, F32 = jnp.bfloat16, jnp.float32


def coords():
    dp = lax.axis_index("dp"); sh = lax.axis_index("shard")
    core = sh % 2; yhi = (sh // 2) % 2; x = sh // 4
    ylo = dp % 2; z = dp // 2
    return {"x": x, "y": yhi * 2 + ylo, "z": z}, core

def device(c, core):
    return (c["z"] * 2 + c["y"] % 2, c["x"] * 4 + (c["y"] // 2) * 2 + core)

def moved(c, axis, by):
    d = dict(c); d[axis] = (c[axis] + by + 4) % 4
    return d

def block(ref, c, free):
    full = slice(None)
    z = full if "z" in free else c["z"]
    x = full if "x" in free else c["x"]
    ylo = full if "y" in free else c["y"] % 2
    yhi = full if "y" in free else c["y"] // 2
    return ref.at[z, ylo, x, yhi]

class Gather:
    def __init__(self, w, ssem, rsem, dsem_s, dsem_r):
        self.w, self.ssem, self.rsem, self.ds, self.dr = w, ssem, rsem, dsem_s, dsem_r
        self.c, self.core = coords()
        self.sent = []

    def part(self, t, k, core=None):
        core = self.core if core is None else core
        return self.w.at[t * 6 + core * 3 + k]

    def copy(self, t, k, f, s, by, origin):
        order = ORDERS[k]
        b = block(self.part(t, k), origin, order[:f])
        if s == 1:
            b = b.at[..., pl.ds(0 if by == 1 else 128, 128)]
        i = (((t * 3 + k) * 3 + f) * 2 + (s if by != 2 else 1)) * 2 + (1 if by == -1 else 0)
        return pltpu.make_async_remote_copy(
            src_ref=b, dst_ref=b, send_sem=self.ssem.at[i], recv_sem=self.rsem.at[i],
            device_id=device(moved(self.c, order[f], by), self.core), device_id_type=MESH)

    def send(self, t, f, s):
        for k in range(3):
            for by in (1, -1, 2) if f == 0 else (1, -1):
                origin = self.c if s == 0 else moved(self.c, ORDERS[k][f], -by)
                cp = self.copy(t, k, f, s, by, origin)
                cp.start()
                self.sent.append(cp)

    def recv(self, t, f, s):
        for k in range(3):
            for by in (1, -1, 2) if f == 0 else (1, -1):
                self.copy(t, k, f, s, by, moved(self.c, ORDERS[k][f], -(1 + s) * by)).wait_recv()

    def d2d(self, t, k, j, core):
        order = ORDERS[k]
        b = block(self.part(t, k, core), moved(self.c, order[2], (0, -1, 1, 2)[j]), order[:2])
        i = (t * 3 + k) * 4 + j
        return pltpu.make_async_remote_copy(
            src_ref=b, dst_ref=b, send_sem=self.ds.at[i], recv_sem=self.dr.at[i],
            device_id=device(self.c, 1 - self.core), device_id_type=MESH)

    def give(self, t, js):
        for k in range(3):
            for j in js:
                cp = self.d2d(t, k, j, self.core); cp.start(); self.sent.append(cp)

    def take(self, t):
        for k in range(3):
            for j in range(4):
                self.d2d(t, k, j, 1 - self.core).wait_recv()

    def step(self, t, n):
        if n > 0:
            self.recv(t, *PLAN[n - 1])
        if n < 5:
            self.send(t, *PLAN[n])
        if n == 3:
            self.give(t, (0,))
        if n == 4:
            self.give(t, (1, 2))
        if n == 5:
            self.give(t, (3,))

    def finish(self):
        for cp in self.sent:
            cp.wait_send()

def neighbours(c, core):
    out = [device(c, 1 - core)]
    for axis in ("x", "y", "z"):
        for by in (1, -1):
            out.append(device(moved(c, axis, by), core))
    return out + [device(moved(c, axis, 2), core) for axis in ("x", "y", "z")]

def barrier(c, core):
    sem = pltpu.get_barrier_semaphore()
    for d in neighbours(c, core):
        pl.semaphore_signal(sem, inc=1, device_id=d, device_id_type=MESH)
    pl.semaphore_wait(sem, 10)

def both_rows(own, other, core):
    a, b = own[...].astype(F32), other[...].astype(F32)
    return jnp.concatenate([jnp.where(core == 0, a, b), jnp.where(core == 0, b, a)], axis=0)


def merge(t, own_q, other_q, own_o, other_o, w, c, core):
    if t == 2:
        cols = both_rows(own_o, other_o, core)
    else:
        a = both_rows(own_q, other_q, core)
        starts = [96 * (8 * t + 2 * g + e) + 48 * half for half in range(2) for e in range(2) for g in range(4)]
        starts += [1536 + 96 * (4 * t + h) + 48 * half for half in range(2) for h in range(4)]
        v = 2304 + 384 * t
        cols = jnp.concatenate([a[:, n : n + 48] for n in starts] + [a[:, v : v + 384]], axis=1)
    for k in range(3):
        part = jnp.where(core == 0, cols[:, 256 * k : 256 * k + 256], cols[:, 768 + 256 * k : 1024 + 256 * k])
        w[t * 6 + core * 3 + k, c["z"], c["y"] % 2, c["x"], c["y"] // 2] = part.astype(BF)


def gain_tile(gain, core):
    g = gain[...].astype(F32)
    zero = jnp.zeros((1, 116), F32)
    row = jnp.where(core == 0, jnp.concatenate([g, zero], axis=1),
                    jnp.concatenate([zero[:, :12], g, zero[:, :104]], axis=1))
    first = lax.broadcasted_iota(jnp.int32, (8, 128), 0) == 0
    return jnp.where(first, jnp.broadcast_to(row, (8, 128)), 0.0).astype(BF)


def angles(freq, clen, cos, sin):
    def put(start, size, at):
        a = at.astype(F32) * freq[...]
        rows = pl.ds(start, size)
        cos[rows, :] = jnp.concatenate([jnp.cos(a)[:, :48]] * 8, axis=1)
        sin[rows, :] = jnp.concatenate([jnp.sin(a)[:, :48]] * 8, axis=1)

    @pl.loop(0, 16)
    def _(i):
        put(pl.multiple_of(i * 48, 16), 48, lax.broadcasted_iota(jnp.int32, (48, 128), 0) + i * 48)

    row = lax.broadcasted_iota(jnp.int32, (16, 128), 0)
    at = jnp.zeros((16, 128), jnp.int32)
    for r in range(8):
        at = jnp.where(row == r, clen[r], at)
    put(768, 16, at)


class GainRing:
    def __init__(self, g, ssem, rsem):
        self.g, self.ssem, self.rsem = g, ssem, rsem
        self.c, self.core = coords()
        self.sent = []

    def copy(self, f, by, origin):
        order = ORDERS[0]
        b = block(self.g, origin, order[:f])
        i = f * 4 + by + 1
        return pltpu.make_async_remote_copy(
            src_ref=b, dst_ref=b, send_sem=self.ssem.at[i], recv_sem=self.rsem.at[i],
            device_id=device(moved(self.c, order[f], by), self.core), device_id_type=MESH)

    def step(self, n):
        if n > 0:
            for by in (1, -1, 2):
                self.copy(n - 1, by, moved(self.c, ORDERS[0][n - 1], -by)).wait_recv()
        if n < 3:
            for by in (1, -1, 2):
                cp = self.copy(n, by, self.c)
                cp.start()
                self.sent.append(cp)

    def finish(self):
        for cp in self.sent:
            cp.wait_send()


def gain_row(g):
    tiles = g[...].astype(F32).reshape(64, 8, 128)
    values = jnp.sum(tiles, axis=1).astype(BF)
    column = lax.broadcasted_iota(jnp.int32, (64, 1536), 1)
    chip = lax.broadcasted_iota(jnp.int32, (64, 1536), 0) * 24
    mine = jnp.where((column >= chip) & (column < chip + 24), 1.0, 0.0).astype(BF)
    spread = lax.dot_general(values, mine, (((0,), (0,)), ((), ())), preferred_element_type=F32)
    n = lax.broadcasted_iota(jnp.int32, (128, 1536), 1).astype(F32)
    within = n - 24.0 * jnp.floor((n + 0.5) * (1.0 / 24.0))
    j = lax.broadcasted_iota(jnp.int32, (128, 1536), 0).astype(F32)
    return jnp.sum(jnp.where(within == j, spread, 0.0), axis=0, keepdims=True)


def normalize(xb, nb, gain):
    def scaled(start, size):
        wide = xb[pl.ds(start, size), :].astype(F32)
        factor = lax.rsqrt(jnp.mean(wide * wide, axis=-1, keepdims=True) + EPS)
        return wide * factor * gain

    @pl.loop(0, 12)
    def _(i):
        start = pl.multiple_of(i * 64, 64)
        nb[pl.ds(start, 64), :] = scaled(start, 64).astype(BF)

    nb[768:784, :] = jnp.concatenate([scaled(768, 8), jnp.zeros((8, 1536), F32)], axis=0).astype(BF)


def project(nb, w, u, t, core):
    @pl.loop(0, 3)
    def _(i):
        j = core * 3 + i
        rhs = w[t * 6 + j].reshape(1536, 256)
        u[:, pl.ds(pl.multiple_of(j * 256, 256), 256)] = jnp.dot(nb[...], rhs, preferred_element_type=F32)


def heads(u, cos, sin, qe, qo, kp, vp, t):
    def turned(lo, half, r, c, s):
        a, b = u[r, lo : lo + half], u[r, lo + half : lo + 2 * half]
        return (a * c - b * s).astype(BF), (b * c + a * s).astype(BF)

    def packed(a, b, lo):
        return jnp.concatenate([a[:, lo : lo + 96], b[:, lo : lo + 96], a[:, lo + 96 : lo + 192], b[:, lo + 96 : lo + 192]], axis=1)

    @pl.loop(0, 7)
    def _(i):
        r = pl.ds(pl.multiple_of(i * 112, 16), 112)
        c, s = cos[r, :], sin[r, :]
        a, b = turned(0, 384, r, c, s)
        qe[t, r, :] = packed(a, b, 0)
        qo[t, r, :] = packed(a, b, 192)
        a, b = turned(768, 192, r, c[:, :192], s[:, :192])
        kp[t, r, :] = packed(a, b, 0)
        vp[t, r, :] = u[r, 1152:1536].astype(BF)


def attend(qe, qo, kp, vp, attn, g):
    t, pair, j = g // 4, g % 4 // 2, g % 2
    win = slice(128 * pair, 128 * pair + 256)
    base = 64 * pair + 48 * j
    lane = lax.broadcasted_iota(jnp.int32, (16, 256), 1)
    mine = ((lane >= base) & (lane < base + 48)) | ((lane >= base + 96) & (lane < base + 144))
    mine = jnp.where(mine, 1.0, 0.0).astype(BF)[:1]
    off = 96 * (g % 4) - 128 * pair
    for i in range(3):
        lo, n = 256 * i, 256 * (i + 1)
        q = jnp.concatenate([qe[t, lo:n, win] * mine, qo[t, lo:n, win] * mine], axis=0)
        s = lax.dot_general(q, kp[t, 0:n, win], (((1,), (1,)), ((), ())), preferred_element_type=F32)
        row = lax.broadcasted_iota(jnp.int32, (512, 256), 0) & 255
        column = lax.broadcasted_iota(jnp.int32, (512, 256), 1)
        last = jnp.where(column <= row, s[:, lo:n], NEGATIVE)
        s = jnp.concatenate([s[:, :lo], last], axis=1) if i else last
        e = jnp.exp2(s * RATE - jnp.max(s, axis=-1, keepdims=True) * RATE)
        total = jnp.sum(e, axis=-1, keepdims=True)
        o = jnp.dot(e.astype(BF), vp[t, 0:n, win], preferred_element_type=F32)
        o = (o * (1.0 / total)).astype(BF)[:, off : off + 96]
        attn[lo:n, 192 * g : 192 * g + 192] = jnp.concatenate([o[:256], o[256:]], axis=1)


def decode_rows(ref, t, g):
    lo = 192 * (g // 2) + 48 * (g % 2)
    rows = jnp.concatenate([ref[t, 768:784, lo : lo + 48], ref[t, 768:784, lo + 96 : lo + 144]], axis=1)
    return rows.astype(F32)[:8]


def decode_queries(qe, qo):
    return jnp.stack([decode_rows((qe, qo)[h % 2], h // 8, h % 8 // 2) for h in range(16)])


def decode_block(qe, qo, kc, vc, clen, pk):
    q = decode_queries(qe, qo)
    lane = lax.broadcasted_iota(jnp.int32, (16, 768), 1)
    first = (lax.broadcasted_iota(jnp.int32, (16, 768), 0) // 2) * 96
    mine = (lane >= first) & (lane < first + 96)
    at = lax.axis_index("shard") * 512 + lax.broadcasted_iota(jnp.int32, (16, 512), 1)
    for r in range(8):
        one = q[:, r, :]
        spread = jnp.concatenate([one] * 8, axis=1)
        qw = jnp.where(mine, spread, 0.0).astype(BF)
        s = lax.dot_general(qw, kc[r], (((1,), (1,)), ((), ())), preferred_element_type=F32) * SCALE
        live = at < clen[r]
        s = jnp.where(live, s, NEGATIVE)
        peak = jnp.max(s, axis=-1, keepdims=True)
        e = jnp.where(live, jnp.exp(s - peak), 0.0)
        total = jnp.sum(e, axis=-1, keepdims=True)
        every = jnp.where(mine, jnp.dot(e.astype(BF), vc[r], preferred_element_type=F32), 0.0)
        acc = every[:, 0:96]
        for g in range(1, 8):
            acc = acc + every[:, 96 * g : 96 * g + 96]
        pk[:, r, :] = jnp.concatenate(
            [acc, jnp.broadcast_to(peak, (16, 16)), jnp.broadcast_to(total, (16, 16))], axis=1)


class Combine:
    def __init__(self, pk, rv, ssem, rsem):
        self.pk, self.rv, self.ssem, self.rsem = pk, rv, ssem, rsem
        self.sent = []

    def copy(self, j):
        c, core = coords()
        return pltpu.make_async_remote_copy(
            src_ref=self.pk.at[j], dst_ref=self.rv.at[j], send_sem=self.ssem.at[j], recv_sem=self.rsem.at[j],
            device_id=partner(c, core, j), device_id_type=MESH)

    def send(self, j):
        cp = self.copy(j)
        cp.start()
        self.sent.append(cp)

    def add(self, j):
        self.copy(j).wait_recv()
        a, b = self.pk[j], self.rv[j]
        pa, pb = a[:, :, 96:97], b[:, :, 96:97]
        top = jnp.maximum(pa, pb)
        both = a * jnp.exp(pa - top) + b * jnp.exp(pb - top)
        lane = lax.broadcasted_iota(jnp.int32, both.shape, 2)
        self.pk[j + 1] = jnp.where((lane >= 96) & (lane < 112), top, both)

    def finish(self):
        for cp in self.sent:
            cp.wait_send()


def partner(c, core, j):
    if j == 0:
        return device(c, 1 - core)
    if j == 1:
        return device(moved(c, "y", 2), core)
    if j == 2:
        return device({**c, "x": c["x"] + 1 - 2 * (c["x"] % 2)}, core)
    return device(moved(c, "x", 2), core)


def decode_mix(pk, qe, qo, kp, vp, attn):
    a = pk[4]
    acc, peak, total = a[:, :, 0:96], a[:, :, 96:97], a[:, :, 112:113]
    q = decode_queries(qe, qo)
    keys = jnp.stack([decode_rows(kp, h // 8, h % 8 // 2) for h in range(16)])
    values = jnp.stack([vp[h // 8, 768:784, 96 * (h % 8 // 2) : 96 * (h % 8 // 2) + 96].astype(F32)[:8] for h in range(16)])
    own = jnp.sum(q * keys, axis=-1, keepdims=True) * SCALE
    top = jnp.maximum(peak, own)
    old, new = jnp.exp(peak - top), jnp.exp(own - top)
    mix = (acc * old + new * values) / (total * old + new)
    zero = jnp.zeros((8, 96), F32)
    for h in range(16):
        attn[768:784, 96 * h : 96 * h + 96] = jnp.concatenate([mix[h], zero], axis=0).astype(BF)


def kernel(wq_ref, wo_ref, gain_ref, x_ref, dx_ref, freq, k_ref, v_ref, clen, out_ref, dout_ref,
           own_q, own_o, other_q, other_o, gown, gother, w, g, xb, nb, u, cos, sin, qe, qo, kp, vp, attn, kc, vc, o, pk, rv,
           ssem, rsem, ds, dr, ps, pr, gs, gr, cs, cr, lsem, osem):
    c, core = coords()
    loads = [pltpu.make_async_copy(s, d, lsem.at[i]) for i, (s, d) in enumerate((
        (wq_ref, own_q), (wo_ref, own_o), (x_ref, xb.at[pl.ds(0, 768)]), (dx_ref, xb.at[pl.ds(768, 8)]),
        (k_ref, kc), (v_ref, vc)))]
    for cp in loads[:2]:
        cp.start()
    gown[...] = gain_tile(gain_ref, core)
    barrier(c, core)
    pre = [pltpu.make_async_remote_copy(
        src_ref=s, dst_ref=d, send_sem=ps.at[i], recv_sem=pr.at[i],
        device_id=device(c, 1 - core), device_id_type=MESH)
        for i, (s, d) in enumerate(((wq_ref, other_q), (wo_ref, other_o), (gown, gother)))]
    for cp in pre:
        cp.start()
    for cp in loads[:2]:
        cp.wait()
    for cp in pre:
        cp.wait()
    g[c["z"], c["y"] % 2, c["x"], c["y"] // 2] = (gown[...].astype(F32) + gother[...].astype(F32)).astype(BF)
    G = Gather(w, ssem, rsem, ds, dr)
    R = GainRing(g, gs, gr)
    D = Combine(pk, rv, cs, cr)

    def ticks(tick):
        if tick < 4:
            R.step(tick)
        for t in range(N_CHUNK):
            if tick == t:
                merge(t, own_q, other_q, own_o, other_o, w, c, core)
            if tick >= t:
                G.step(t, tick - t)

    for tick in range(4):
        ticks(tick)
        if tick == 2:
            for cp in loads[2:]:
                cp.start()
    angles(freq, clen, cos, sin)
    ticks(4)
    for cp in loads[2:4]:
        cp.wait()
    normalize(xb, nb, gain_row(g))
    G.step(0, 5)
    project(nb, w, u, 0, core)
    G.step(1, 4)
    G.step(2, 3)
    G.take(0)
    project(nb, w, u, 0, 1 - core)
    G.step(1, 5)
    heads(u, cos, sin, qe, qo, kp, vp, 0)
    G.step(2, 4)
    attend(qe, qo, kp, vp, attn, 0)
    project(nb, w, u, 1, core)
    G.step(2, 5)
    G.take(1)
    project(nb, w, u, 1, 1 - core)
    heads(u, cos, sin, qe, qo, kp, vp, 1)
    for cp in loads[4:]:
        cp.wait()
    decode_block(qe, qo, kc, vc, clen, pk.at[0])
    for j, groups in enumerate(((1, 2), (3, 4), (5, 6), (7,))):
        D.send(j)
        for g_ in groups:
            attend(qe, qo, kp, vp, attn, g_)
        D.add(j)
    decode_mix(pk, qe, qo, kp, vp, attn)
    G.take(2)

    def leaving(j):
        cols = pl.ds(pl.multiple_of(j * 256, 256), 256)
        return pltpu.make_async_copy(o.at[pl.ds(0, 768), cols], out_ref.at[:, cols], osem.at[j])

    @pl.loop(0, 6)
    def _(j):
        rhs = w[12 + j].reshape(1536, 256)
        o[:, pl.ds(pl.multiple_of(j * 256, 256), 256)] = jnp.dot(
            attn[...], rhs, preferred_element_type=F32).astype(BF)
        leaving(j).start()

    outs = [leaving(j) for j in range(6)]
    outs.append(pltpu.make_async_copy(o.at[pl.ds(768, 8)], dout_ref, osem.at[6]))
    outs[6].start()
    G.finish()
    R.finish()
    D.finish()
    for cp in outs:
        cp.wait()


def per_device(prefill_x, decode_x, norm_gain, wqkv, wo, k_cache, v_cache, cache_len):
    freq = np.power(np.float32(THETA), -np.arange(48, dtype=np.float32) * np.float32(2.0 / HD))
    freq = jnp.asarray(np.pad(freq.astype(np.float32)[None], ((0, 0), (0, 80))))
    hbm, vmem = pl.BlockSpec(memory_space=pl.ANY), pl.BlockSpec(memory_space=pltpu.VMEM)
    n = N_CHUNK
    dma = pltpu.SemaphoreType.DMA
    out, dout = pl.pallas_call(
        kernel,
        out_shape=(jax.ShapeDtypeStruct((768, 1536), BF), jax.ShapeDtypeStruct((8, 1536), BF)),
        in_specs=[hbm, hbm, vmem, hbm, hbm, vmem, hbm, hbm, pl.BlockSpec(memory_space=pltpu.SMEM)],
        out_specs=(hbm, hbm),
        scratch_shapes=[
            pltpu.VMEM((12, 3072), BF), pltpu.VMEM((12, 1536), BF), pltpu.VMEM((12, 3072), BF), pltpu.VMEM((12, 1536), BF),
            pltpu.VMEM((8, 128), BF), pltpu.VMEM((8, 128), BF),
            pltpu.VMEM((6 * n, 4, 2, 4, 2, 24, 256), BF), pltpu.VMEM((4, 2, 4, 2, 8, 128), BF),
            pltpu.VMEM((784, 1536), BF), pltpu.VMEM((784, 1536), BF), pltpu.VMEM((784, 1536), F32),
            pltpu.VMEM((784, 384), F32), pltpu.VMEM((784, 384), F32),
            pltpu.VMEM((2, 784, 384), BF), pltpu.VMEM((2, 784, 384), BF),
            pltpu.VMEM((2, 784, 384), BF), pltpu.VMEM((2, 784, 384), BF),
            pltpu.VMEM((784, 1536), BF), pltpu.VMEM((8, 512, 768), BF), pltpu.VMEM((8, 512, 768), BF),
            pltpu.VMEM((784, 1536), BF), pltpu.VMEM((5, 16, 8, 128), F32), pltpu.VMEM((4, 16, 8, 128), F32),
            dma((36 * n,)), dma((36 * n,)), dma((12 * n,)), dma((12 * n,)), dma((3,)), dma((3,)),
            dma((12,)), dma((12,)), dma((4,)), dma((4,)), dma((6,)), dma((7,)),
        ],
        compiler_params=pltpu.CompilerParams(
            collective_id=0, has_side_effects=True, vmem_limit_bytes=67043328),
        name="sublayer",
    )(wqkv, wo, norm_gain.reshape(1, 12), prefill_x, decode_x, freq, k_cache, v_cache, cache_len)
    return out, dout


def solution(mesh):
    rows = P(("dp", "shard"), None)
    in_specs = (rows, P("dp", None), P(("dp", "shard")), rows, rows,
                P("dp", "shard", None), P("dp", "shard", None), P("dp"))
    return jax.shard_map(per_device, mesh=mesh, in_specs=in_specs,
                         out_specs=(rows, P("dp", None)), check_vma=False)
```
